32 devices in a mesh: section: 2 (over core), expert: 8 (over z, x), head: 2 (over y).
Axes of the slice: x: 2, y: 2, z: 4, core: 2. Of those that a mesh axis runs over, the one named last changes fastest.
Arguments:
- boundary: bfloat16 [2, 2, 1024, 768], P('section', None, 'expert', 'head'), may hold values from -6 to 6
- norm_gain: float32 [2, 768], P('section'), may hold values from 0.25 to 1.75
- gate_prob: float32 [2, 2, 1024], P('section', None, 'expert'), may hold values from 0.25 to 1
- expert_ids: int32 [2, 2, 1024], P('section', None, 'expert'), may hold values from 0 to 7, as said below
- slot_ids: int32 [2, 2, 1024], P('section', None, 'expert'), may hold values from 0 to 32, as said below
- weight_in: bfloat16 [2, 8, 768, 3072], P('section', 'expert', None, 'head'), may hold values from -0.21875 to 0.21875
- weight_out: bfloat16 [2, 8, 3072, 768], P('section', 'expert', 'head'), may hold values from -0.109375 to 0.109375
Outputs:
- boundary_out: bfloat16 [2, 2, 1024, 768], P('section', None, 'expert', 'head')
- grad_in: bfloat16 [2, 8, 768, 3072], P('section', 'expert', None, 'head')
- grad_out: bfloat16 [2, 8, 3072, 768], P('section', 'expert', 'head')
The draws below stay inside these ranges and needn't reach their ends.
Inputs may be any that keep to these rules, and one draw needn't show every extreme that they name: `expert_ids`: within each layer and micro-batch, tokens are taken in blocks of 128 (the tokens of one index of expert); in every block one expert, the same for all blocks of that layer and micro-batch, is named by more than 32 tokens. `slot_ids`: A token's slot is the number of earlier tokens of its block that name the same expert, capped at 32; 32 means the token is dropped. So at most 32 tokens of a block hold a slot below 32 at one expert, and in every layer and micro-batch one expert has all 32 slots filled from every block.
All inputs are finite; a program needn't handle non-finite values.
Results may differ from the reference program's by a relative error of at most 0.008.
Values may be sent and summed in bfloat16 or wider, within the bound.
A program may use at most 128 MiB of HBM per device.

```python
import jax
import jax.numpy as jnp
from jax import lax

D = 768
FF = 3072
TOK_DEV = 128
MICRO = 2
EXPERTS = 8
TOKENS = 1024
CAP = 32


def routing(key):
    block_count = TOKENS // TOK_DEV
    streams = jax.random.split(jax.random.fold_in(key, 11), 3)
    favored = jax.random.randint(streams[0], (2, MICRO, 1, 1), 0, EXPERTS)
    random_ids = jax.random.randint(streams[1], (2, MICRO, block_count, TOK_DEV), 0, EXPERTS)
    position = jnp.arange(TOK_DEV, dtype=jnp.int32)
    chosen = jnp.where(position < CAP + 1, favored, random_ids)
    shuffle_score = jax.random.randint(streams[2], (2, MICRO, block_count, TOK_DEV), 0, 2 ** 18) * 4096 + position
    shuffle = jnp.argsort(shuffle_score, axis=-1)
    route_ids = jnp.take_along_axis(chosen, shuffle, axis=-1)
    onehot = (route_ids[..., None] == jnp.arange(EXPERTS, dtype=jnp.int32)).astype(jnp.int32)
    earlier = jnp.sum((jnp.cumsum(onehot, axis=-2) - onehot) * onehot, axis=-1)
    slot_rank = jnp.minimum(earlier, CAP)
    return (route_ids.reshape(2, MICRO, TOKENS).astype(jnp.int32), slot_rank.reshape(2, MICRO, TOKENS).astype(jnp.int32))


def draw_expert_ids(key, part):
    return routing(key)[0]


def draw_slot_ids(key, part):
    return routing(key)[1]


def shard_levels(key, dims, shards, smallest, largest):
    def one(dim, shards_of):
        heights = jax.random.uniform(jax.random.fold_in(jax.random.fold_in(key, 6), dim), (shards_of,), jnp.float32, smallest / len(shards), largest / len(shards))
        return jnp.repeat(jnp.exp(heights), dims[dim] // shards_of).reshape((-1,) + (1,) * (len(dims) - dim - 1))

    factor_of = one(*shards[0])
    for cut in shards[1:]:
        factor_of = factor_of * one(*cut)
    return factor_of


def noise(own_key, extent, deviation, limit, cuts=(), kind=jnp.bfloat16):
    array = deviation * jax.random.normal(own_key, extent, jnp.float32)
    if cuts:
        array = array * shard_levels(own_key, extent, cuts, -0.22, 0.18)
    return jnp.clip(array, -limit, limit).astype(kind)


def setup_inputs(seed: int = 0) -> dict:
    seeds = jax.random.split(jax.random.key(seed), 8)
    boundary = noise(seeds[0], (2, MICRO, TOKENS, D), 1.0, 6.0, ((0, 2), (2, 8), (3, 2)))
    norm_gain = jnp.clip(1.0 + 0.15 * jax.random.normal(seeds[1], (2, D), jnp.float32), 0.25, 1.75)
    gate_prob = jnp.clip(0.25 + 0.75 * jax.random.uniform(seeds[2], (2, MICRO, TOKENS), jnp.float32) ** shard_levels(seeds[2], (2, MICRO, TOKENS), ((0, 2), (2, 8)), -0.2, 0.2), 0.25, 1.0)
    expert_ids = draw_expert_ids(jax.random.fold_in(seeds[7], 71), 0)
    slot_ids = draw_slot_ids(jax.random.fold_in(seeds[7], 71), 0)
    weight_in = noise(seeds[5], (2, EXPERTS, D, FF), D ** -0.5, 0.21875, ((0, 2), (1, 8), (3, 2)))
    weight_out = noise(seeds[6], (2, EXPERTS, FF, D), FF ** -0.5, 0.109375, ((0, 2), (1, 8), (2, 2)))
    return {"boundary": boundary, "norm_gain": norm_gain, "gate_prob": gate_prob, "expert_ids": expert_ids, "slot_ids": slot_ids, "weight_in": weight_in, "weight_out": weight_out}


EPSILON = 1e-06
ROOT_COEF = 0.7978845608
CUBE_COEF = 0.044715

def activate(pre_act):
    tangent = jnp.tanh(ROOT_COEF * (pre_act + CUBE_COEF * pre_act * pre_act * pre_act))
    act_value = 0.5 * pre_act * (1.0 + tangent)
    act_slope = 0.5 * (1.0 + tangent) + 0.5 * pre_act * (1.0 - tangent * tangent) * ROOT_COEF * (1.0 + 3.0 * CUBE_COEF * pre_act * pre_act)
    return (act_value, act_slope)

def rounded(values):
    return lax.optimization_barrier(values.astype(jnp.bfloat16)).astype(jnp.float32)

def placement_rows(slot_ids):
    block_of = jnp.arange(TOKENS, dtype=jnp.int32) // TOK_DEV
    kept_mask = slot_ids < CAP
    row_of = jnp.where(kept_mask, block_of * CAP + slot_ids, TOKENS // TOK_DEV * CAP).astype(jnp.int32)
    return (kept_mask, row_of)

def dispatch(tokens, expert_ids, row_of):
    buffer = jnp.zeros((EXPERTS, TOKENS // TOK_DEV * CAP, D), tokens.dtype)
    return buffer.at[expert_ids, row_of].set(tokens, mode='drop')

def collect(buffer, expert_ids, row_of, kept_mask):
    last_row = buffer.shape[1] - 1
    picked = buffer[expert_ids, jnp.minimum(row_of, last_row)]
    return jnp.where(kept_mask[:, None], picked.astype(jnp.float32), jnp.float32(0.0))

def normalize(rows_in, gain):
    values = rows_in.astype(jnp.float32)
    inv_scale = lax.rsqrt(lax.optimization_barrier(jnp.mean(values * values, axis=-1, keepdims=True)) + EPSILON)
    return (values * inv_scale * gain).astype(jnp.bfloat16)

def layer_forward(tokens, gain, weight_in, weight_out, expert_ids, slot_ids, gate_prob):
    kept_mask, row_of = placement_rows(slot_ids)
    buffer = dispatch(tokens, expert_ids, row_of)
    half_ff = FF // 2

    def per_expert(operands):
        rows_in, first_weight, second_weight = operands
        normed = normalize(rows_in, gain)
        pre_act = jnp.dot(normed, first_weight, preferred_element_type=jnp.float32)
        act_value = activate(pre_act)[0].astype(jnp.bfloat16)
        part_low = jnp.dot(act_value[:, :half_ff], second_weight[:half_ff], preferred_element_type=jnp.float32)
        part_high = jnp.dot(act_value[:, half_ff:], second_weight[half_ff:], preferred_element_type=jnp.float32)
        return (rounded(part_low) + rounded(part_high)).astype(jnp.bfloat16)
    outputs = lax.map(per_expert, (buffer, weight_in, weight_out))
    combined = collect(outputs, expert_ids, row_of, kept_mask)
    return (tokens.astype(jnp.float32) + gate_prob[:, None] * combined).astype(jnp.bfloat16)

def layer_backward(tokens, grad_tok, gain, weight_in, weight_out, expert_ids, slot_ids, gate_prob):
    kept_mask, row_of = placement_rows(slot_ids)
    buffer = dispatch(tokens, expert_ids, row_of)
    sent_grad = (gate_prob[:, None] * grad_tok.astype(jnp.float32)).astype(jnp.bfloat16)
    grad_buffer = dispatch(sent_grad, expert_ids, row_of)
    half_ff = FF // 2

    def per_expert(operands):
        rows_in, grad_rows, first_weight, second_weight = operands
        normed = normalize(rows_in, gain)
        pre_act = jnp.dot(normed, first_weight, preferred_element_type=jnp.float32)
        act_slope = activate(pre_act)[1]
        grad_act = jnp.dot(grad_rows, second_weight.T, preferred_element_type=jnp.float32)
        grad_pre = (grad_act * act_slope).astype(jnp.bfloat16)
        part_low = jnp.dot(grad_pre[:, :half_ff], first_weight[:, :half_ff].T, preferred_element_type=jnp.float32)
        part_high = jnp.dot(grad_pre[:, half_ff:], first_weight[:, half_ff:].T, preferred_element_type=jnp.float32)
        return (rounded(part_low) + rounded(part_high)).astype(jnp.bfloat16)
    grad_normed = lax.map(per_expert, (buffer, grad_buffer, weight_in, weight_out))
    grad_back = collect(grad_normed, expert_ids, row_of, kept_mask)
    values = tokens.astype(jnp.float32)
    inv_scale = lax.rsqrt(lax.optimization_barrier(jnp.mean(values * values, axis=-1, keepdims=True)) + EPSILON)
    scaled_grad = gain * grad_back
    cross_sum = lax.optimization_barrier(jnp.sum(scaled_grad * values, axis=-1, keepdims=True))
    result = grad_tok.astype(jnp.float32) + inv_scale * scaled_grad - values * inv_scale * inv_scale * inv_scale * cross_sum / D
    return result.astype(jnp.bfloat16)

def layer_gradients(inputs, cotangents, gain, weight_in, weight_out, expert_ids, slot_ids, gate_prob):
    row_buffers = []
    grad_buffers = []
    for micro_index in range(MICRO):
        kept_mask, row_of = placement_rows(slot_ids[micro_index])
        row_buffers.append(dispatch(inputs[micro_index], expert_ids[micro_index], row_of))
        sent_grad = (gate_prob[micro_index][:, None] * cotangents[micro_index].astype(jnp.float32)).astype(jnp.bfloat16)
        grad_buffers.append(dispatch(sent_grad, expert_ids[micro_index], row_of))
    rows_all = jnp.stack(row_buffers, axis=1)
    grads_all = jnp.stack(grad_buffers, axis=1)

    def per_expert(operands):
        rows_each, grads_each, first_weight, second_weight = operands
        total_in = jnp.zeros((D, FF), jnp.float32)
        total_out = jnp.zeros((FF, D), jnp.float32)
        for micro_index in range(MICRO):
            normed = normalize(rows_each[micro_index], gain)
            pre_act = jnp.dot(normed, first_weight, preferred_element_type=jnp.float32)
            act_value, act_slope = activate(pre_act)
            grad_act = jnp.dot(grads_each[micro_index], second_weight.T, preferred_element_type=jnp.float32)
            grad_pre = (grad_act * act_slope).astype(jnp.bfloat16)
            total_in = total_in + jnp.dot(normed.T, grad_pre, preferred_element_type=jnp.float32)
            total_out = total_out + jnp.dot(act_value.astype(jnp.bfloat16).T, grads_each[micro_index], preferred_element_type=jnp.float32)
        return (total_in.astype(jnp.bfloat16), total_out.astype(jnp.bfloat16))
    return lax.map(per_expert, (rows_all, grads_all, weight_in, weight_out))

def reference(boundary, norm_gain, gate_prob, expert_ids, slot_ids, weight_in, weight_out):
    hiddens = []
    tops = []
    grad_hiddens = []
    bottoms = []
    for micro_index in range(MICRO):
        hidden = layer_forward(boundary[0, micro_index], norm_gain[0], weight_in[0], weight_out[0], expert_ids[0, micro_index], slot_ids[0, micro_index], gate_prob[0, micro_index])
        top_out = layer_forward(hidden, norm_gain[1], weight_in[1], weight_out[1], expert_ids[1, micro_index], slot_ids[1, micro_index], gate_prob[1, micro_index])
        grad_hidden = layer_backward(hidden, boundary[1, micro_index], norm_gain[1], weight_in[1], weight_out[1], expert_ids[1, micro_index], slot_ids[1, micro_index], gate_prob[1, micro_index])
        bottom = layer_backward(boundary[0, micro_index], grad_hidden, norm_gain[0], weight_in[0], weight_out[0], expert_ids[0, micro_index], slot_ids[0, micro_index], gate_prob[0, micro_index])
        hiddens.append(hidden)
        tops.append(top_out)
        grad_hiddens.append(grad_hidden)
        bottoms.append(bottom)
    boundary_out = jnp.stack([jnp.stack(bottoms), jnp.stack(tops)])
    lower_in, lower_out = layer_gradients(boundary[0], jnp.stack(grad_hiddens), norm_gain[0], weight_in[0], weight_out[0], expert_ids[0], slot_ids[0], gate_prob[0])
    upper_in, upper_out = layer_gradients(jnp.stack(hiddens), boundary[1], norm_gain[1], weight_in[1], weight_out[1], expert_ids[1], slot_ids[1], gate_prob[1])
    return (boundary_out, jnp.stack([lower_in, upper_in]), jnp.stack([lower_out, upper_out]))
```

```python
import functools

import jax
import jax.numpy as jnp
from jax import lax
from jax.experimental import pallas as pl
from jax.experimental.pallas import tpu as pltpu
from jax.sharding import PartitionSpec as P

EPSILON = 1e-06
ROOT_COEF = 0.7978845608
CUBE_COEF = 0.044715
MESH = pl.DeviceIdType.MESH
BF16 = jnp.bfloat16
F32 = jnp.float32
FWD, BWD = 0, 1
COLS = 256
SPLIT = 2
VMEM_LIMIT = 56 * 2**20
COPY_LIMIT = 2**20
RELAYED = {"f0": False, "b1": True, "f1": False, "b0": False}


def activate(pre_act):
    tangent = jnp.tanh(ROOT_COEF * (pre_act + CUBE_COEF * pre_act * pre_act * pre_act))
    act_value = 0.5 * pre_act * (1.0 + tangent)
    act_slope = 0.5 * (1.0 + tangent) + 0.5 * pre_act * (1.0 - tangent * tangent) * ROOT_COEF * (
        1.0 + 3.0 * CUBE_COEF * pre_act * pre_act
    )
    return (act_value, act_slope)


def dot(left, right, dims=((1,), (0,))):
    return lax.dot_general(left, right, (dims, ((), ())), preferred_element_type=F32)


NT = ((1,), (1,))
TN = ((0,), (0,))


def kernel(
    experts, cap, pad, relayed,
    local_ref, gain_ref, prob_ref, ids_ref, slots_ref, win_hbm, wout_hbm,
    out_ref, gin_ref, gout_ref,
    tab, tab2, send, rows, normed, act, gpre, mid, inv_ref, keep, away, recvp, back,
    sec_src, sec_in, xsend, xrecv, route, route_in, win_ref, wout_ref, load_sem, turn,
    s1, r1, s2, r2, s3, r3, s4, r4, s5, r5, s6, r6, s7, s8, r8,
):
    win_load = pltpu.make_async_copy(win_hbm, win_ref, load_sem.at[0])
    wout_load = pltpu.make_async_copy(wout_hbm, wout_ref, load_sem.at[1])
    win_load.start()
    wout_load.start()
    sec, me, head = lax.axis_index("section"), lax.axis_index("expert"), lax.axis_index("head")
    other = 1 - head
    upper = lax.div(2 * me, experts)
    micro, tok, half = local_ref.shape
    full = 2 * half
    total = experts * pad
    groups = total // tok
    piece_rows = total // SPLIT
    hidden_half = win_ref.shape[1]
    chunks = hidden_half // COLS
    own_cols = pl.ds(pl.multiple_of(head * half, 128), half)
    other_cols = pl.ds(pl.multiple_of(other * half, 128), half)

    barrier = pltpu.get_barrier_semaphore()

    def greet(k, carry):
        d = lax.rem(me + k, experts)
        for h in range(2):
            pl.semaphore_signal(
                barrier, inc=1, device_id={"expert": d, "head": h}, device_id_type=MESH
            )
        return carry

    lax.fori_loop(1, experts, greet, 0)
    pl.semaphore_signal(barrier, inc=1, device_id={"head": other}, device_id_type=MESH)
    pl.semaphore_signal(barrier, inc=1, device_id={"section": 1 - sec}, device_id_type=MESH)

    def far_first(k):
        return k * upper + (experts - 1 - k) * (1 - upper)

    def near_first(k):
        return far_first(experts - 1 - k)

    def each(order, action, with_me, lo=0, hi=experts):
        def step(k, carry):
            d = order(k)
            if with_me:
                action(d)
            else:
                pl.when(d != me)(lambda: action(d))
            return carry

        lax.fori_loop(lo, hi, step, 0)

    def slot_rows(index):
        return pl.ds(pl.multiple_of(index * pad, pad), pad)

    def micro_rows(m, index):
        return pl.ds(pl.multiple_of(m * total + index * pad, pad), pad)

    def span(m):
        return slice(m * total, (m + 1) * total)

    eye = lax.broadcasted_iota(jnp.int32, (tok, tok), 0) == lax.broadcasted_iota(
        jnp.int32, (tok, tok), 1
    )

    def to_col(row):
        return jnp.sum(jnp.where(eye, row, 0.0), axis=1, keepdims=True)

    def to_row(col):
        return jnp.sum(jnp.where(eye, col, 0.0), axis=0, keepdims=True)

    def fill_tab(ref, m, target):
        place_of = lax.broadcasted_iota(jnp.int32, (total, tok), 0).astype(F32)
        ref[m] = jnp.where(target == place_of, 1.0, 0.0).astype(BF16)

    for m in range(micro):
        ids, slots = ids_ref[m : m + 1, :], slots_ref[m : m + 1, :]
        target = jnp.where(slots < cap, ids * pad + slots, -1).astype(F32)
        fill_tab(tab, m, target)
        route[m : m + 1, :] = target
        route[micro + m : micro + m + 1, :] = prob_ref[m : m + 1, :]
    prob = [to_col(prob_ref[m : m + 1, :]) for m in range(micro)]
    gain = gain_ref[...]

    route_copy = pltpu.make_async_remote_copy(
        src_ref=route,
        dst_ref=route_in,
        send_sem=s8,
        recv_sem=r8,
        device_id={"section": 1 - sec},
        device_id_type=MESH,
    )

    def route_done():
        route_copy.wait_recv()
        for m in range(micro):
            fill_tab(tab2, m, route_in[m : m + 1, :])

    HOME, AWAY = 0, 1

    def target_section(slot):
        return sec if slot == HOME else 1 - sec

    def chunk_copy(slot, kind, m, dst, came_from):
        return pltpu.make_async_remote_copy(
            src_ref=send.at[slot, m, slot_rows(dst), :],
            dst_ref=rows.at[kind, micro_rows(m, came_from), own_cols],
            send_sem=s1.at[slot, m],
            recv_sem=r1.at[kind, m, came_from],
            device_id={"section": target_section(slot), "expert": dst},
            device_id_type=MESH,
        )

    def cross_copy(slot, kind, m, dst, came_from, cols):
        return pltpu.make_async_remote_copy(
            src_ref=send.at[slot, m, slot_rows(dst), :],
            dst_ref=rows.at[kind, micro_rows(m, came_from), cols],
            send_sem=s2.at[slot, m],
            recv_sem=r2.at[kind, m, came_from],
            device_id={"section": target_section(slot), "expert": dst, "head": other},
            device_id_type=MESH,
        )

    def relay_copy(kind, m, block, cols):
        return pltpu.make_async_remote_copy(
            src_ref=rows.at[kind, micro_rows(m, block), cols],
            dst_ref=rows.at[kind, micro_rows(m, block), cols],
            send_sem=s7.at[kind, m],
            recv_sem=r2.at[kind, m, block],
            device_id={"head": other},
            device_id_type=MESH,
        )

    def place(slot, m, tokens):
        table = tab if slot == HOME else tab2
        send[slot, m] = dot(table[m], tokens).astype(BF16)

    def dispatch(slot, kind, m, relay):
        def both_heads(d):
            chunk_copy(slot, kind, m, d, me).start()
            if not relay:
                cross_copy(slot, kind, m, d, me, own_cols).start()

        each(far_first, both_heads, slot == AWAY)
        if slot == HOME:
            rows[kind, micro_rows(m, me), own_cols] = send[slot, m, slot_rows(me), :]
            if not relay:
                cross_copy(slot, kind, m, me, me, own_cols).start()

    def arrived(slot, kind, m, relay):
        def one(block):
            chunk_copy(slot, kind, m, block, block).wait_recv()
            if relay:
                relay_copy(kind, m, block, own_cols).start()

        if slot == HOME and relay:
            relay_copy(kind, m, me, own_cols).start()
        each(near_first, one, slot == AWAY)
        each(
            near_first,
            lambda block: cross_copy(slot, kind, m, block, block, other_cols).wait_recv(),
            True,
        )

    def sent(slot, kind, m, relay):
        blocks = experts if slot == AWAY else experts - 1
        pltpu.make_async_remote_copy(
            src_ref=send.at[slot, m, 0 : blocks * pad, :],
            dst_ref=rows.at[kind, 0 : blocks * pad, own_cols],
            send_sem=s1.at[slot, m],
            recv_sem=r1.at[kind, m, 0],
            device_id={"head": other},
            device_id_type=MESH,
        ).wait_send()
        if not relay:
            pltpu.make_async_remote_copy(
                src_ref=send.at[slot, m],
                dst_ref=rows.at[kind, 0:total, own_cols],
                send_sem=s2.at[slot, m],
                recv_sem=r2.at[kind, m, 0],
                device_id={"head": other},
                device_id_type=MESH,
            ).wait_send()

    def relay_sent(kind, m):
        pltpu.make_async_remote_copy(
            src_ref=rows.at[kind, 0:total, own_cols],
            dst_ref=rows.at[kind, 0:total, own_cols],
            send_sem=s7.at[kind, m],
            recv_sem=r2.at[kind, m, 0],
            device_id={"head": other},
            device_id_type=MESH,
        ).wait_send()

    def piece_at(c):
        p = c * upper + (SPLIT - 1 - c) * (1 - upper)
        return p, pl.ds(pl.multiple_of(p * piece_rows, piece_rows), piece_rows)

    def piece_of(m, c):
        p, _ = piece_at(c)
        return pl.ds(pl.multiple_of(m * total + p * piece_rows, piece_rows), piece_rows)

    def away_copy(kind, m, c):
        _, part = piece_at(c)
        return pltpu.make_async_remote_copy(
            src_ref=away.at[kind, m, part, :],
            dst_ref=recvp.at[kind, m, part, :],
            send_sem=s3.at[kind, m, c],
            recv_sem=r3.at[kind, m, c],
            device_id={"head": other},
            device_id_type=MESH,
        )

    def back_copy(kind, m, dst, came_from):
        return pltpu.make_async_remote_copy(
            src_ref=keep.at[kind, m, slot_rows(dst), :],
            dst_ref=back.at[kind, m, slot_rows(came_from), :],
            send_sem=s4.at[kind, m],
            recv_sem=r4.at[kind, m, came_from],
            device_id={"expert": dst},
            device_id_type=MESH,
        )

    def back_sent(kind, m):
        pltpu.make_async_remote_copy(
            src_ref=keep.at[kind, m, 0 : (experts - 1) * pad, :],
            dst_ref=back.at[kind, m, 0 : (experts - 1) * pad, :],
            send_sem=s4.at[kind, m],
            recv_sem=r4.at[kind, m, 0],
            device_id={"head": other},
            device_id_type=MESH,
        ).wait_send()

    def send_back(kind, m):
        if kind == BWD:
            sum_copy(m).wait_recv()
        for c in range(SPLIT):
            p, part = piece_at(c)
            away_copy(kind, m, c).wait_recv()
            if kind == FWD:
                summed = keep[kind, m, part, :].astype(F32) + recvp[kind, m, part, :].astype(F32)
                keep[kind, m, part, :] = summed.astype(BF16)
            else:
                for i in range(groups // SPLIT):
                    g = p * (groups // SPLIT) + i
                    here = pl.ds(pl.multiple_of(g * tok, tok), tok)
                    there = pl.ds(pl.multiple_of(m * total + g * tok, tok), tok)
                    cross = to_col(xsend[m, pl.ds(g, 1), :] + xrecv[m, pl.ds(g, 1), :])
                    inv = inv_ref[there, :]
                    grad = keep[kind, m, here, :].astype(F32) + recvp[kind, m, here, :].astype(F32)
                    values = rows[FWD, there, own_cols].astype(F32)
                    delta = inv * (gain_ref[:, own_cols] * grad) - values * (
                        inv * inv * inv * cross / full
                    )
                    keep[kind, m, here, :] = delta.astype(BF16)
            each(
                far_first,
                lambda dst: back_copy(kind, m, dst, me).start(),
                False,
                c * experts // SPLIT,
                (c + 1) * experts // SPLIT,
            )
        back[kind, m, slot_rows(me), :] = keep[kind, m, slot_rows(me), :]

    def collect(kind, m):
        each(near_first, lambda block: back_copy(kind, m, block, block).wait_recv(), False)
        return dot(tab[m], back[kind, m], TN)

    def section_copy(m):
        return pltpu.make_async_remote_copy(
            src_ref=sec_src.at[m],
            dst_ref=sec_in.at[m],
            send_sem=s5.at[m],
            recv_sem=r5.at[m],
            device_id={"section": 1 - sec},
            device_id_type=MESH,
        )

    def sum_copy(m):
        return pltpu.make_async_remote_copy(
            src_ref=xsend.at[m],
            dst_ref=xrecv.at[m],
            send_sem=s6.at[m],
            recv_sem=r6.at[m],
            device_id={"head": other},
            device_id_type=MESH,
        )

    def normalize(m):
        values = rows[FWD, span(m), :].astype(F32)
        inv_scale = lax.rsqrt(jnp.mean(values * values, axis=-1, keepdims=True) + EPSILON)
        inv_ref[span(m), :] = inv_scale
        normed[span(m), :] = (values * inv_scale * gain).astype(BF16)

    def each_chunk(action):
        def step(c, carry):
            action(pl.ds(pl.multiple_of(c * COLS, COLS), COLS))
            return carry

        lax.fori_loop(0, chunks, step, 0)

    def out_partial(m):
        for c in range(SPLIT):
            _, part = piece_at(c)
            away[FWD, m, part, :] = dot(act[piece_of(m, c), :], wout_ref[:, other_cols]).astype(
                BF16
            )
            away_copy(FWD, m, c).start()
        keep[FWD, m] = dot(act[span(m), :], wout_ref[:, own_cols]).astype(BF16)

    def grad_partial(m):
        for c in range(SPLIT):
            _, part = piece_at(c)
            away[BWD, m, part, :] = dot(gpre[piece_of(m, c), :], win_ref[other_cols, :], NT).astype(
                BF16
            )
            away_copy(BWD, m, c).start()
        keep[BWD, m] = dot(gpre[span(m), :], win_ref[own_cols, :], NT).astype(BF16)
        for g in range(groups):
            here = slice(g * tok, (g + 1) * tok)
            there = slice(m * total + g * tok, m * total + (g + 1) * tok)
            cross = jnp.zeros((tok, 1), F32)
            for ref, cols in ((away, other_cols), (keep, own_cols)):
                scaled = ref[BWD, m, here, :].astype(F32) * gain_ref[:, cols]
                cross = cross + jnp.sum(
                    scaled * rows[FWD, there, cols].astype(F32), axis=1, keepdims=True
                )
            xsend[m, g : g + 1, :] = to_row(cross)
        sum_copy(m).start()

    def layer_out(m, tokens):
        return (tokens.astype(F32) + prob[m] * collect(FWD, m)).astype(BF16)

    def sent_grad(weight, cot):
        return (weight * cot.astype(F32)).astype(BF16)

    def layer_grad(m, cot):
        return (cot.astype(F32) + collect(BWD, m)).astype(BF16)

    def in_grads():
        def first(c, carry):
            part = pl.ds(pl.multiple_of(c * COLS, COLS), COLS)
            gin_ref[part, :] = dot(normed[:, part], gpre[...], TN).astype(BF16)
            return carry

        lax.fori_loop(0, full // COLS, first, 0)

    def out_grads():
        def second(part):
            gout_ref[part, :] = dot(act[:, part], rows[BWD], TN).astype(BF16)

        each_chunk(second)

    @pl.when(sec == 0)
    def _():
        own_fwd, own_bwd, their_fwd = relayed["f0"], relayed["b0"], relayed["f1"]
        for m in range(micro):
            place(HOME, m, local_ref[m])
        pl.semaphore_wait(barrier, 2 * experts)
        dispatch(HOME, FWD, 0, own_fwd)
        route_copy.start()
        win_load.wait()
        wout_load.wait()

        def forward(m):
            arrived(HOME, FWD, m, own_fwd)
            pl.semaphore_signal(
                turn.at[m], inc=1, device_id={"section": 1 - sec}, device_id_type=MESH
            )
            if m + 1 < micro:
                dispatch(HOME, FWD, m + 1, own_fwd)
            normalize(m)

            def chunk(part):
                pre = dot(normed[span(m), :], win_ref[:, part])
                value, slope = activate(pre)
                act[span(m), part] = value.astype(BF16)
                mid[span(m), part] = slope.astype(mid.dtype)

            each_chunk(chunk)

        def hidden(m):
            sec_src[m] = layer_out(m, local_ref[m])
            place(AWAY, m, sec_src[m])
            dispatch(AWAY, FWD, m, their_fwd)
            section_copy(m).start()

        forward(0)
        out_partial(0)
        route_done()
        forward(1)
        send_back(FWD, 0)
        out_partial(1)
        hidden(0)
        send_back(FWD, 1)
        hidden(1)

        def backward(m):
            arrived(AWAY, BWD, m, own_bwd)

            def chunk(part):
                grad_act = dot(rows[BWD, span(m), :], wout_ref[part, :], NT)
                gpre[span(m), part] = (grad_act * mid[span(m), part].astype(F32)).astype(BF16)

            each_chunk(chunk)

        backward(0)
        grad_partial(0)
        backward(1)
        send_back(BWD, 0)
        grad_partial(1)
        out_grads()
        send_back(BWD, 1)
        section_copy(0).wait_recv()
        out_ref[0] = layer_grad(0, sec_in[0])
        in_grads()
        section_copy(1).wait_recv()
        out_ref[1] = layer_grad(1, sec_in[1])

        for m in range(micro):
            sent(HOME, FWD, m, own_fwd)
            sent(AWAY, FWD, m, their_fwd)
            if own_fwd:
                relay_sent(FWD, m)
            if own_bwd:
                relay_sent(BWD, m)

    @pl.when(sec != 0)
    def _():
        own_bwd, own_fwd, their_bwd = relayed["b1"], relayed["f1"], relayed["b0"]
        for m in range(micro):
            place(HOME, m, sent_grad(prob[m], local_ref[m]))
        pl.semaphore_wait(barrier, 2 * experts)
        route_copy.start()
        win_load.wait()
        wout_load.wait()

        def early_grad(m):
            pl.semaphore_wait(turn.at[m], 1)
            dispatch(HOME, BWD, m, own_bwd)
            arrived(HOME, BWD, m, own_bwd)

            def early(part):
                grad_act = dot(rows[BWD, span(m), :], wout_ref[part, :], NT)
                mid[span(m), part] = grad_act.astype(mid.dtype)

            each_chunk(early)

        early_grad(0)
        route_done()
        prob_in = [to_col(route_in[micro + m : micro + m + 1, :]) for m in range(micro)]
        early_grad(1)

        def both(m):
            arrived(AWAY, FWD, m, own_fwd)
            normalize(m)

            def chunk(part):
                pre = dot(normed[span(m), :], win_ref[:, part])
                value, slope = activate(pre)
                act[span(m), part] = value.astype(BF16)
                gpre[span(m), part] = (mid[span(m), part].astype(F32) * slope).astype(BF16)

            each_chunk(chunk)

        def finish(m):
            sec_src[m] = layer_grad(m, local_ref[m])
            place(AWAY, m, sent_grad(prob_in[m], sec_src[m]))
            dispatch(AWAY, BWD, m, their_bwd)
            section_copy(m).start()

        both(0)
        grad_partial(0)
        both(1)
        send_back(BWD, 0)
        grad_partial(1)
        finish(0)
        send_back(BWD, 1)
        out_partial(0)
        out_partial(1)
        finish(1)
        in_grads()
        out_grads()
        send_back(FWD, 0)
        send_back(FWD, 1)
        for m in range(micro):
            section_copy(m).wait_recv()
            out_ref[m] = layer_out(m, sec_in[m])

        for m in range(micro):
            sent(HOME, BWD, m, own_bwd)
            sent(AWAY, BWD, m, their_bwd)
            if own_fwd:
                relay_sent(FWD, m)
            if own_bwd:
                relay_sent(BWD, m)

    for m in range(micro):
        for kind in (FWD, BWD):
            back_sent(kind, m)
            for c in range(SPLIT):
                away_copy(kind, m, c).wait_send()
        section_copy(m).wait_send()
        sum_copy(m).wait_send()
    route_copy.wait_send()


def copy_out(out_in, gin_in, gout_in, out_ref, gin_ref, gout_ref, sem):
    pairs = ((gin_in, gin_ref), (gout_in, gout_ref), (out_in, out_ref))
    copies = [pltpu.make_async_copy(a, b, sem.at[i]) for i, (a, b) in enumerate(pairs)]
    for copy in copies:
        copy.start()
    for copy in copies:
        copy.wait()


def on_device(boundary, norm_gain, gate_prob, expert_ids, slot_ids, weight_in, weight_out):
    experts = lax.axis_size("expert")
    micro, tok, half = boundary.shape[1:]
    full, hidden_half = weight_in.shape[2:]
    cap = 2 * tok // experts
    pad = -(-cap // 16) * 16
    total = experts * pad
    mid_type = F32 if total <= 512 else BF16
    vmem = pl.BlockSpec(memory_space=pltpu.VMEM)
    anywhere = pl.BlockSpec(memory_space=pl.ANY)
    per_block = pltpu.SemaphoreType.DMA((2, micro, experts))
    per_pair = pltpu.SemaphoreType.DMA((2, micro))
    per_piece = pltpu.SemaphoreType.DMA((2, micro, SPLIT))
    per_micro = pltpu.SemaphoreType.DMA((micro,))
    pieces = pltpu.VMEM((2, micro, total, half), BF16)
    tokens = pltpu.VMEM((micro, tok, half), BF16)
    sums = pltpu.VMEM((micro, max(8, total // tok), tok), F32)
    routes = pltpu.VMEM((8, tok), F32)
    table = pltpu.VMEM((micro, total, tok), BF16)
    out, grad_in, grad_out = pl.pallas_call(
        functools.partial(kernel, experts, cap, pad, RELAYED),
        out_shape=(
            pltpu.VMEM((micro, tok, half), BF16),
            pltpu.VMEM((full, hidden_half), BF16),
            pltpu.VMEM((hidden_half, full), BF16),
        ),
        in_specs=[vmem] * 5 + [anywhere] * 2,
        out_specs=(vmem, vmem, vmem),
        scratch_shapes=[
            table,
            table,
            pieces,
            pltpu.VMEM((2, micro * total, full), BF16),
            pltpu.VMEM((micro * total, full), BF16),
            pltpu.VMEM((micro * total, hidden_half), BF16),
            pltpu.VMEM((micro * total, hidden_half), BF16),
            pltpu.VMEM((micro * total, hidden_half), mid_type),
            pltpu.VMEM((micro * total, 1), F32),
            pieces,
            pieces,
            pieces,
            pieces,
            tokens,
            tokens,
            sums,
            sums,
            routes,
            routes,
            pltpu.VMEM((full, hidden_half), BF16),
            pltpu.VMEM((hidden_half, full), BF16),
            pltpu.SemaphoreType.DMA((2,)),
            pltpu.SemaphoreType.REGULAR((micro,)),
            per_pair, per_block,
            per_pair, per_block,
            per_piece, per_piece,
            per_pair, per_block,
            per_micro, per_micro,
            per_micro, per_micro,
            per_pair,
            pltpu.SemaphoreType.DMA,
            pltpu.SemaphoreType.DMA,
        ],
        compiler_params=pltpu.CompilerParams(
            collective_id=0, has_side_effects=True, vmem_limit_bytes=VMEM_LIMIT
        ),
    )(
        boundary[0], norm_gain, gate_prob[0], expert_ids[0], slot_ids[0],
        weight_in[0, 0], weight_out[0, 0],
    )
    results = (out, grad_in, grad_out)
    out, grad_in, grad_out = pl.pallas_call(
        copy_out,
        out_shape=[jax.ShapeDtypeStruct(x.shape, x.dtype) for x in results],
        in_specs=[vmem] * 3,
        out_specs=[anywhere] * 3,
        scratch_shapes=[pltpu.SemaphoreType.DMA((3,))],
        compiler_params=pltpu.CompilerParams(vmem_limit_bytes=COPY_LIMIT),
    )(*results)
    return (out[None], grad_in[None, None], grad_out[None, None])


def solution(mesh):
    placed = (
        P("section", None, "expert", "head"),
        P("section", None),
        P("section", None, "expert"),
        P("section", None, "expert"),
        P("section", None, "expert"),
        P("section", "expert", None, "head"),
        P("section", "expert", "head", None),
    )
    return jax.shard_map(
        on_device,
        mesh=mesh,
        in_specs=placed,
        out_specs=(
            P("section", None, "expert", "head"),
            P("section", "expert", None, "head"),
            P("section", "expert", "head", None),
        ),
        check_vma=False,
    )
```

```python
import functools

import jax
import jax.numpy as jnp
from jax import lax
from jax.experimental import pallas as pl
from jax.experimental.pallas import tpu as pltpu
from jax.sharding import PartitionSpec as P

EPSILON = 1e-06
ROOT_COEF = 0.7978845608
CUBE_COEF = 0.044715
MESH = pl.DeviceIdType.MESH
BF16 = jnp.bfloat16
F32 = jnp.float32
FWD, BWD = 0, 1
COLS = 256
SPLIT = 2
VMEM_LIMIT = 56 * 2**20
COPY_LIMIT = 2**20
RELAYED = {"f0": (True, True), "b1": (True, True), "f1": (True, False), "b0": (True, False)}
RELAY_NEAR = True
TURN_AT = 0
HOLD = 1
ORDER = 2
UNROLL = 6
PUMP_AT = 0


def activate(pre_act):
    tangent = jnp.tanh(ROOT_COEF * (pre_act + CUBE_COEF * pre_act * pre_act * pre_act))
    act_value = 0.5 * pre_act * (1.0 + tangent)
    act_slope = 0.5 * (1.0 + tangent) + 0.5 * pre_act * (1.0 - tangent * tangent) * ROOT_COEF * (
        1.0 + 3.0 * CUBE_COEF * pre_act * pre_act
    )
    return (act_value, act_slope)


def dot(left, right, dims=((1,), (0,))):
    return lax.dot_general(left, right, (dims, ((), ())), preferred_element_type=F32)


NT = ((1,), (1,))
TN = ((0,), (0,))


def kernel(
    experts, cap, pad, relayed,
    local_ref, gain_ref, prob_ref, ids_ref, slots_ref, win_hbm, wout_hbm,
    out_ref, gin_ref, gout_ref,
    tab, tab2, send, rows, normed, act, gpre, mid, inv_ref, keep, away, recvp, back,
    sec_src, sec_in, xsend, xrecv, route, route_in, win_ref, wout_ref, load_sem, turn,
    s1, r1, s2, r2, s3, r3, s4, r4, s5, r5, s6, r6, s7, s8, r8,
):
    win_load = pltpu.make_async_copy(win_hbm, win_ref, load_sem.at[0])
    wout_load = pltpu.make_async_copy(wout_hbm, wout_ref, load_sem.at[1])
    win_load.start()
    wout_load.start()
    sec, me, head = lax.axis_index("section"), lax.axis_index("expert"), lax.axis_index("head")
    other = 1 - head
    upper = lax.div(2 * me, experts)
    micro, tok, half = local_ref.shape
    full = 2 * half
    total = experts * pad
    groups = total // tok
    piece_rows = total // SPLIT
    hidden_half = win_ref.shape[1]
    chunks = hidden_half // COLS
    own_cols = pl.ds(pl.multiple_of(head * half, 128), half)
    other_cols = pl.ds(pl.multiple_of(other * half, 128), half)

    barrier = pltpu.get_barrier_semaphore()

    def greet(k, carry):
        d = lax.rem(me + k, experts)
        for h in range(2):
            pl.semaphore_signal(
                barrier, inc=1, device_id={"expert": d, "head": h}, device_id_type=MESH
            )
        return carry

    lax.fori_loop(1, experts, greet, 0)
    pl.semaphore_signal(barrier, inc=1, device_id={"head": other}, device_id_type=MESH)
    pl.semaphore_signal(barrier, inc=1, device_id={"section": 1 - sec}, device_id_type=MESH)

    def far_first(k):
        return k * upper + (experts - 1 - k) * (1 - upper)

    def near_first(k):
        return far_first(experts - 1 - k)

    def each(order, action, with_me, lo=0, hi=experts):
        def step(k, carry):
            d = order(k)
            if with_me:
                action(d)
            else:
                pl.when(d != me)(lambda: action(d))
            return carry

        lax.fori_loop(lo, hi, step, 0)

    def slot_rows(index):
        return pl.ds(pl.multiple_of(index * pad, pad), pad)

    def micro_rows(m, index):
        return pl.ds(pl.multiple_of(m * total + index * pad, pad), pad)

    def span(m):
        return slice(m * total, (m + 1) * total)

    eye = lax.broadcasted_iota(jnp.int32, (tok, tok), 0) == lax.broadcasted_iota(
        jnp.int32, (tok, tok), 1
    )

    def to_col(row):
        return jnp.sum(jnp.where(eye, row, 0.0), axis=1, keepdims=True)

    def to_row(col):
        return jnp.sum(jnp.where(eye, col, 0.0), axis=0, keepdims=True)

    def fill_tab(ref, m, target):
        place_of = lax.broadcasted_iota(jnp.int32, (total, tok), 0).astype(F32)
        ref[m] = jnp.where(target == place_of, 1.0, 0.0).astype(BF16)

    for m in range(micro):
        ids, slots = ids_ref[m : m + 1, :], slots_ref[m : m + 1, :]
        target = jnp.where(slots < cap, ids * pad + slots, -1).astype(F32)
        fill_tab(tab, m, target)
        route[m : m + 1, :] = target
        route[micro + m : micro + m + 1, :] = prob_ref[m : m + 1, :]
    prob = [to_col(prob_ref[m : m + 1, :]) for m in range(micro)]
    gain = gain_ref[...]

    route_copy = pltpu.make_async_remote_copy(
        src_ref=route,
        dst_ref=route_in,
        send_sem=s8,
        recv_sem=r8,
        device_id={"section": 1 - sec},
        device_id_type=MESH,
    )

    def route_done():
        route_copy.wait_recv()
        for m in range(micro):
            fill_tab(tab2, m, route_in[m : m + 1, :])

    HOME, AWAY = 0, 1

    def target_section(slot):
        return sec if slot == HOME else 1 - sec

    def chunk_copy(slot, kind, m, dst, came_from):
        return pltpu.make_async_remote_copy(
            src_ref=send.at[slot, m, slot_rows(dst), :],
            dst_ref=rows.at[kind, micro_rows(m, came_from), own_cols],
            send_sem=s1.at[slot, m],
            recv_sem=r1.at[kind, m, came_from],
            device_id={"section": target_section(slot), "expert": dst},
            device_id_type=MESH,
        )

    def cross_copy(slot, kind, m, dst, came_from, cols):
        return pltpu.make_async_remote_copy(
            src_ref=send.at[slot, m, slot_rows(dst), :],
            dst_ref=rows.at[kind, micro_rows(m, came_from), cols],
            send_sem=s2.at[slot, m],
            recv_sem=r2.at[kind, m, came_from],
            device_id={"section": target_section(slot), "expert": dst, "head": other},
            device_id_type=MESH,
        )

    def relay_copy(kind, m, block, cols):
        return pltpu.make_async_remote_copy(
            src_ref=rows.at[kind, micro_rows(m, block), cols],
            dst_ref=rows.at[kind, micro_rows(m, block), cols],
            send_sem=s7.at[kind, m],
            recv_sem=r2.at[kind, m, block],
            device_id={"head": other},
            device_id_type=MESH,
        )

    def place(slot, m, tokens):
        table = tab if slot == HOME else tab2
        send[slot, m] = dot(table[m], tokens).astype(BF16)

    def dispatch(slot, kind, m, relay):
        def both_heads(d):
            chunk_copy(slot, kind, m, d, me).start()
            if not relay:
                cross_copy(slot, kind, m, d, me, own_cols).start()

        each(near_first if relay and RELAY_NEAR else far_first, both_heads, slot == AWAY)
        if slot == HOME:
            rows[kind, micro_rows(m, me), own_cols] = send[slot, m, slot_rows(me), :]
            if not relay:
                cross_copy(slot, kind, m, me, me, own_cols).start()

    def pump(slot, kind, m, relay):
        def one(block):
            chunk_copy(slot, kind, m, block, block).wait_recv()
            if relay:
                relay_copy(kind, m, block, own_cols).start()

        if slot == HOME and relay:
            relay_copy(kind, m, me, own_cols).start()
        each(near_first, one, slot == AWAY)

    def arrived(slot, kind, m):
        each(
            near_first,
            lambda block: cross_copy(slot, kind, m, block, block, other_cols).wait_recv(),
            True,
        )

    def sent(slot, kind, m, relay):
        blocks = experts if slot == AWAY else experts - 1
        pltpu.make_async_remote_copy(
            src_ref=send.at[slot, m, 0 : blocks * pad, :],
            dst_ref=rows.at[kind, 0 : blocks * pad, own_cols],
            send_sem=s1.at[slot, m],
            recv_sem=r1.at[kind, m, 0],
            device_id={"head": other},
            device_id_type=MESH,
        ).wait_send()
        if not relay:
            pltpu.make_async_remote_copy(
                src_ref=send.at[slot, m],
                dst_ref=rows.at[kind, 0:total, own_cols],
                send_sem=s2.at[slot, m],
                recv_sem=r2.at[kind, m, 0],
                device_id={"head": other},
                device_id_type=MESH,
            ).wait_send()

    def relay_sent(kind, m):
        pltpu.make_async_remote_copy(
            src_ref=rows.at[kind, 0:total, own_cols],
            dst_ref=rows.at[kind, 0:total, own_cols],
            send_sem=s7.at[kind, m],
            recv_sem=r2.at[kind, m, 0],
            device_id={"head": other},
            device_id_type=MESH,
        ).wait_send()

    def piece_at(c):
        p = c * upper + (SPLIT - 1 - c) * (1 - upper)
        return p, pl.ds(pl.multiple_of(p * piece_rows, piece_rows), piece_rows)

    def piece_of(m, c):
        p, _ = piece_at(c)
        return pl.ds(pl.multiple_of(m * total + p * piece_rows, piece_rows), piece_rows)

    def away_copy(kind, m, c):
        _, part = piece_at(c)
        return pltpu.make_async_remote_copy(
            src_ref=away.at[kind, m, part, :],
            dst_ref=recvp.at[kind, m, part, :],
            send_sem=s3.at[kind, m, c],
            recv_sem=r3.at[kind, m, c],
            device_id={"head": other},
            device_id_type=MESH,
        )

    def back_copy(kind, m, dst, came_from):
        return pltpu.make_async_remote_copy(
            src_ref=keep.at[kind, m, slot_rows(dst), :],
            dst_ref=back.at[kind, m, slot_rows(came_from), :],
            send_sem=s4.at[kind, m],
            recv_sem=r4.at[kind, m, came_from],
            device_id={"expert": dst},
            device_id_type=MESH,
        )

    def back_sent(kind, m):
        pltpu.make_async_remote_copy(
            src_ref=keep.at[kind, m, 0 : (experts - 1) * pad, :],
            dst_ref=back.at[kind, m, 0 : (experts - 1) * pad, :],
            send_sem=s4.at[kind, m],
            recv_sem=r4.at[kind, m, 0],
            device_id={"head": other},
            device_id_type=MESH,
        ).wait_send()

    def send_back(kind, m):
        if kind == BWD:
            sum_copy(m).wait_recv()
        for c in range(SPLIT):
            p, part = piece_at(c)
            away_copy(kind, m, c).wait_recv()
            if kind == FWD:
                summed = keep[kind, m, part, :].astype(F32) + recvp[kind, m, part, :].astype(F32)
                keep[kind, m, part, :] = summed.astype(BF16)
            else:
                for i in range(groups // SPLIT):
                    g = p * (groups // SPLIT) + i
                    here = pl.ds(pl.multiple_of(g * tok, tok), tok)
                    there = pl.ds(pl.multiple_of(m * total + g * tok, tok), tok)
                    cross = to_col(xsend[m, pl.ds(g, 1), :] + xrecv[m, pl.ds(g, 1), :])
                    inv = inv_ref[there, :]
                    grad = keep[kind, m, here, :].astype(F32) + recvp[kind, m, here, :].astype(F32)
                    values = rows[FWD, there, own_cols].astype(F32)
                    delta = inv * (gain_ref[:, own_cols] * grad) - values * (
                        inv * inv * inv * cross / full
                    )
                    keep[kind, m, here, :] = delta.astype(BF16)
            each(
                far_first,
                lambda dst: back_copy(kind, m, dst, me).start(),
                False,
                c * experts // SPLIT,
                (c + 1) * experts // SPLIT,
            )
        back[kind, m, slot_rows(me), :] = keep[kind, m, slot_rows(me), :]

    def collect(kind, m):
        each(near_first, lambda block: back_copy(kind, m, block, block).wait_recv(), False)
        return dot(tab[m], back[kind, m], TN)

    def section_copy(m):
        return pltpu.make_async_remote_copy(
            src_ref=sec_src.at[m],
            dst_ref=sec_in.at[m],
            send_sem=s5.at[m],
            recv_sem=r5.at[m],
            device_id={"section": 1 - sec},
            device_id_type=MESH,
        )

    def sum_copy(m):
        return pltpu.make_async_remote_copy(
            src_ref=xsend.at[m],
            dst_ref=xrecv.at[m],
            send_sem=s6.at[m],
            recv_sem=r6.at[m],
            device_id={"head": other},
            device_id_type=MESH,
        )

    def normalize(m):
        values = rows[FWD, span(m), :].astype(F32)
        inv_scale = lax.rsqrt(jnp.mean(values * values, axis=-1, keepdims=True) + EPSILON)
        inv_ref[span(m), :] = inv_scale
        normed[span(m), :] = (values * inv_scale * gain).astype(BF16)

    def each_chunk(action):
        def step(c, carry):
            action(pl.ds(pl.multiple_of(c * COLS, COLS), COLS))
            return carry

        lax.fori_loop(0, chunks, step, 0, unroll=UNROLL if total <= 512 else 1)

    def out_partial(m):
        for c in range(SPLIT):
            _, part = piece_at(c)
            away[FWD, m, part, :] = dot(act[piece_of(m, c), :], wout_ref[:, other_cols]).astype(
                BF16
            )
            away_copy(FWD, m, c).start()
        keep[FWD, m] = dot(act[span(m), :], wout_ref[:, own_cols]).astype(BF16)

    def grad_partial(m):
        for c in range(SPLIT):
            _, part = piece_at(c)
            away[BWD, m, part, :] = dot(gpre[piece_of(m, c), :], win_ref[other_cols, :], NT).astype(
                BF16
            )
            away_copy(BWD, m, c).start()
        keep[BWD, m] = dot(gpre[span(m), :], win_ref[own_cols, :], NT).astype(BF16)
        for g in range(groups):
            here = slice(g * tok, (g + 1) * tok)
            there = slice(m * total + g * tok, m * total + (g + 1) * tok)
            cross = jnp.zeros((tok, 1), F32)
            for ref, cols in ((away, other_cols), (keep, own_cols)):
                scaled = ref[BWD, m, here, :].astype(F32) * gain_ref[:, cols]
                cross = cross + jnp.sum(
                    scaled * rows[FWD, there, cols].astype(F32), axis=1, keepdims=True
                )
            xsend[m, g : g + 1, :] = to_row(cross)
        sum_copy(m).start()

    def layer_out(m, tokens):
        return (tokens.astype(F32) + prob[m] * collect(FWD, m)).astype(BF16)

    def sent_grad(weight, cot):
        return (weight * cot.astype(F32)).astype(BF16)

    def layer_grad(m, cot):
        return (cot.astype(F32) + collect(BWD, m)).astype(BF16)

    def in_grads():
        def first(c, carry):
            part = pl.ds(pl.multiple_of(c * COLS, COLS), COLS)
            gin_ref[part, :] = dot(normed[:, part], gpre[...], TN).astype(BF16)
            return carry

        lax.fori_loop(0, full // COLS, first, 0)

    def out_grads():
        def second(part):
            gout_ref[part, :] = dot(act[:, part], rows[BWD], TN).astype(BF16)

        each_chunk(second)

    @pl.when(sec == 0)
    def _():
        own_fwd, own_bwd, their_fwd = relayed["f0"], relayed["b0"], relayed["f1"]
        for m in range(micro):
            place(HOME, m, local_ref[m])
        pl.semaphore_wait(barrier, 2 * experts)
        dispatch(HOME, FWD, 0, own_fwd[0])
        if own_fwd[1]:
            dispatch(HOME, FWD, 1, own_fwd[1])
        route_copy.start()
        win_load.wait()
        wout_load.wait()
        pump(HOME, FWD, 0, own_fwd[0])

        def signal_turn():
            pl.semaphore_signal(turn, inc=1, device_id={"section": 1 - sec}, device_id_type=MESH)

        if TURN_AT == 0:
            signal_turn()
        if PUMP_AT == 0 and own_fwd[1]:
            pump(HOME, FWD, 1, own_fwd[1])

        def forward(m):
            arrived(HOME, FWD, m)
            if m == 0 and TURN_AT == 1:
                signal_turn()
            if m == 0 and not own_fwd[1]:
                dispatch(HOME, FWD, 1, own_fwd[1])
            normalize(m)

            def chunk(part):
                pre = dot(normed[span(m), :], win_ref[:, part])
                value, slope = activate(pre)
                act[span(m), part] = value.astype(BF16)
                mid[span(m), part] = slope.astype(mid.dtype)

            each_chunk(chunk)

        def hidden(m):
            sec_src[m] = layer_out(m, local_ref[m])
            place(AWAY, m, sec_src[m])
            dispatch(AWAY, FWD, m, their_fwd[m])
            section_copy(m).start()

        forward(0)
        if PUMP_AT == 1 and own_fwd[1]:
            pump(HOME, FWD, 1, own_fwd[1])
        out_partial(0)
        route_done()
        if not own_fwd[1]:
            pump(HOME, FWD, 1, own_fwd[1])
        forward(1)
        send_back(FWD, 0)
        if HOLD:
            signal_turn()
        out_partial(1)
        hidden(0)
        send_back(FWD, 1)
        hidden(1)

        def backward(m):
            pump(AWAY, BWD, m, own_bwd[m])
            arrived(AWAY, BWD, m)

            def chunk(part):
                grad_act = dot(rows[BWD, span(m), :], wout_ref[part, :], NT)
                gpre[span(m), part] = (grad_act * mid[span(m), part].astype(F32)).astype(BF16)

            each_chunk(chunk)

        backward(0)
        grad_partial(0)
        backward(1)
        send_back(BWD, 0)
        grad_partial(1)
        out_grads()
        send_back(BWD, 1)
        section_copy(0).wait_recv()
        out_ref[0] = layer_grad(0, sec_in[0])
        in_grads()
        section_copy(1).wait_recv()
        out_ref[1] = layer_grad(1, sec_in[1])

        for m in range(micro):
            sent(HOME, FWD, m, own_fwd[m])
            sent(AWAY, FWD, m, their_fwd[m])
            if own_fwd[m]:
                relay_sent(FWD, m)
            if own_bwd[m]:
                relay_sent(BWD, m)

    @pl.when(sec != 0)
    def _():
        own_bwd, own_fwd, their_bwd = relayed["b1"], relayed["f1"], relayed["b0"]
        for m in range(micro):
            place(HOME, m, sent_grad(prob[m], local_ref[m]))
        pl.semaphore_wait(barrier, 2 * experts)
        route_copy.start()
        win_load.wait()
        wout_load.wait()

        pl.semaphore_wait(turn, 1)
        for m in range(micro):
            dispatch(HOME, BWD, m, own_bwd[m])
        if HOLD:
            pl.semaphore_wait(turn, 1)
        for m in range(micro):
            pump(HOME, BWD, m, own_bwd[m])

        def early_grad(m):
            arrived(HOME, BWD, m)

            def early(part):
                grad_act = dot(rows[BWD, span(m), :], wout_ref[part, :], NT)
                mid[span(m), part] = grad_act.astype(mid.dtype)

            each_chunk(early)

        early_grad(0)
        route_done()
        prob_in = [to_col(route_in[micro + m : micro + m + 1, :]) for m in range(micro)]
        early_grad(1)

        def both(m):
            arrived(AWAY, FWD, m)
            normalize(m)

            def chunk(part):
                pre = dot(normed[span(m), :], win_ref[:, part])
                value, slope = activate(pre)
                act[span(m), part] = value.astype(BF16)
                gpre[span(m), part] = (mid[span(m), part].astype(F32) * slope).astype(BF16)

            each_chunk(chunk)

        def finish(m):
            sec_src[m] = layer_grad(m, local_ref[m])
            place(AWAY, m, sent_grad(prob_in[m], sec_src[m]))
            dispatch(AWAY, BWD, m, their_bwd[m])
            section_copy(m).start()

        pump(AWAY, FWD, 0, own_fwd[0])
        both(0)
        grad_partial(0)
        if ORDER == 0:
            pump(AWAY, FWD, 1, own_fwd[1])
            both(1)
            send_back(BWD, 0)
            grad_partial(1)
            finish(0)
        if ORDER == 1:
            send_back(BWD, 0)
            pump(AWAY, FWD, 1, own_fwd[1])
            both(1)
            finish(0)
            grad_partial(1)
        if ORDER == 2:
            send_back(BWD, 0)
            pump(AWAY, FWD, 1, own_fwd[1])
            both(1)
            grad_partial(1)
            finish(0)
        if ORDER == 3:
            if own_fwd[1]:
                pump(AWAY, FWD, 1, own_fwd[1])
            send_back(BWD, 0)
            if not own_fwd[1]:
                pump(AWAY, FWD, 1, own_fwd[1])
            both(1)
            finish(0)
            grad_partial(1)
        send_back(BWD, 1)
        out_partial(0)
        out_partial(1)
        finish(1)
        in_grads()
        out_grads()
        send_back(FWD, 0)
        send_back(FWD, 1)
        for m in range(micro):
            section_copy(m).wait_recv()
            out_ref[m] = layer_out(m, sec_in[m])

        for m in range(micro):
            sent(HOME, BWD, m, own_bwd[m])
            sent(AWAY, BWD, m, their_bwd[m])
            if own_fwd[m]:
                relay_sent(FWD, m)
            if own_bwd[m]:
                relay_sent(BWD, m)

    for m in range(micro):
        for kind in (FWD, BWD):
            back_sent(kind, m)
            for c in range(SPLIT):
                away_copy(kind, m, c).wait_send()
        section_copy(m).wait_send()
        sum_copy(m).wait_send()
    route_copy.wait_send()


def copy_out(out_in, gin_in, gout_in, out_ref, gin_ref, gout_ref, sem):
    pairs = ((gin_in, gin_ref), (gout_in, gout_ref), (out_in, out_ref))
    copies = [pltpu.make_async_copy(a, b, sem.at[i]) for i, (a, b) in enumerate(pairs)]
    for copy in copies:
        copy.start()
    for copy in copies:
        copy.wait()


def on_device(boundary, norm_gain, gate_prob, expert_ids, slot_ids, weight_in, weight_out):
    experts = lax.axis_size("expert")
    micro, tok, half = boundary.shape[1:]
    full, hidden_half = weight_in.shape[2:]
    cap = 2 * tok // experts
    pad = -(-cap // 16) * 16
    total = experts * pad
    mid_type = F32 if total <= 512 else BF16
    vmem = pl.BlockSpec(memory_space=pltpu.VMEM)
    anywhere = pl.BlockSpec(memory_space=pl.ANY)
    per_block = pltpu.SemaphoreType.DMA((2, micro, experts))
    per_pair = pltpu.SemaphoreType.DMA((2, micro))
    per_piece = pltpu.SemaphoreType.DMA((2, micro, SPLIT))
    per_micro = pltpu.SemaphoreType.DMA((micro,))
    pieces = pltpu.VMEM((2, micro, total, half), BF16)
    tokens = pltpu.VMEM((micro, tok, half), BF16)
    sums = pltpu.VMEM((micro, max(8, total // tok), tok), F32)
    routes = pltpu.VMEM((8, tok), F32)
    table = pltpu.VMEM((micro, total, tok), BF16)
    out, grad_in, grad_out = pl.pallas_call(
        functools.partial(kernel, experts, cap, pad, RELAYED),
        out_shape=(
            pltpu.VMEM((micro, tok, half), BF16),
            pltpu.VMEM((full, hidden_half), BF16),
            pltpu.VMEM((hidden_half, full), BF16),
        ),
        in_specs=[vmem] * 5 + [anywhere] * 2,
        out_specs=(vmem, vmem, vmem),
        scratch_shapes=[
            table,
            table,
            pieces,
            pltpu.VMEM((2, micro * total, full), BF16),
            pltpu.VMEM((micro * total, full), BF16),
            pltpu.VMEM((micro * total, hidden_half), BF16),
            pltpu.VMEM((micro * total, hidden_half), BF16),
            pltpu.VMEM((micro * total, hidden_half), mid_type),
            pltpu.VMEM((micro * total, 1), F32),
            pieces,
            pieces,
            pieces,
            pieces,
            tokens,
            tokens,
            sums,
            sums,
            routes,
            routes,
            pltpu.VMEM((full, hidden_half), BF16),
            pltpu.VMEM((hidden_half, full), BF16),
            pltpu.SemaphoreType.DMA((2,)),
            pltpu.SemaphoreType.REGULAR,
            per_pair, per_block,
            per_pair, per_block,
            per_piece, per_piece,
            per_pair, per_block,
            per_micro, per_micro,
            per_micro, per_micro,
            per_pair,
            pltpu.SemaphoreType.DMA,
            pltpu.SemaphoreType.DMA,
        ],
        compiler_params=pltpu.CompilerParams(
            collective_id=0, has_side_effects=True, vmem_limit_bytes=VMEM_LIMIT
        ),
    )(
        boundary[0], norm_gain, gate_prob[0], expert_ids[0], slot_ids[0],
        weight_in[0, 0], weight_out[0, 0],
    )
    results = (out, grad_in, grad_out)
    out, grad_in, grad_out = pl.pallas_call(
        copy_out,
        out_shape=[jax.ShapeDtypeStruct(x.shape, x.dtype) for x in results],
        in_specs=[vmem] * 3,
        out_specs=[anywhere] * 3,
        scratch_shapes=[pltpu.SemaphoreType.DMA((3,))],
        compiler_params=pltpu.CompilerParams(vmem_limit_bytes=COPY_LIMIT),
    )(*results)
    return (out[None], grad_in[None, None], grad_out[None, None])


def solution(mesh):
    placed = (
        P("section", None, "expert", "head"),
        P("section", None),
        P("section", None, "expert"),
        P("section", None, "expert"),
        P("section", None, "expert"),
        P("section", "expert", None, "head"),
        P("section", "expert", "head", None),
    )
    return jax.shard_map(
        on_device,
        mesh=mesh,
        in_specs=placed,
        out_specs=(
            P("section", None, "expert", "head"),
            P("section", "expert", None, "head"),
            P("section", "expert", "head", None),
        ),
        check_vma=False,
    )
```

```python
import functools

import jax
import jax.numpy as jnp
from jax import lax
from jax.experimental import pallas as pl
from jax.experimental.pallas import tpu as pltpu
from jax.sharding import PartitionSpec as P

EPSILON = 1e-06
ROOT_COEF = 0.7978845608
CUBE_COEF = 0.044715
MESH = pl.DeviceIdType.MESH
BF16 = jnp.bfloat16
F32 = jnp.float32
FWD, BWD = 0, 1
COLS = 256
SPLIT = 2
VMEM_LIMIT = 56 * 2**20
COPY_LIMIT = 2**20
RELAYED = {"f0": (True, True), "b1": (True, True), "f1": (True, False), "b0": (True, False)}
DIRECT = {"f0": (True, True), "b1": (True, False), "f1": (False, False), "b0": (False, True)}
RELAY_NEAR = True
TURN_AT = 0
HOLD = 1
TAIL = 0
ORDER = 3
UNROLL = 6
PUMP_AT = 0


def activate(pre_act):
    tangent = jnp.tanh(ROOT_COEF * (pre_act + CUBE_COEF * pre_act * pre_act * pre_act))
    act_value = 0.5 * pre_act * (1.0 + tangent)
    act_slope = 0.5 * (1.0 + tangent) + 0.5 * pre_act * (1.0 - tangent * tangent) * ROOT_COEF * (
        1.0 + 3.0 * CUBE_COEF * pre_act * pre_act
    )
    return (act_value, act_slope)


def dot(left, right, dims=((1,), (0,))):
    return lax.dot_general(left, right, (dims, ((), ())), preferred_element_type=F32)


NT = ((1,), (1,))
TN = ((0,), (0,))


def kernel(
    experts, cap, pad, relayed, direct,
    local_hbm, gain_hbm, prob_hbm, ids_hbm, slots_hbm, win_hbm, wout_hbm,
    out_ref, gin_ref, gout_ref,
    tab, tab2, send, rows, normed, act, gpre, mid, inv_ref, keep, away, recvp, back,
    sec_src, sec_in, xsend, xrecv, route, route_in, win_ref, wout_ref,
    local_ref, gain_ref, prob_ref, ids_ref, slots_ref, load_sem, turn,
    s1, r1, s2, r2, s3, r3, s4, r4, s5, r5, s6, r6, s7, s8, r8,
):
    small = [
        pltpu.make_async_copy(source, target, load_sem.at[2 + i])
        for i, (source, target) in enumerate(
            (
                (local_hbm, local_ref),
                (gain_hbm, gain_ref),
                (prob_hbm, prob_ref),
                (ids_hbm, ids_ref),
                (slots_hbm, slots_ref),
            )
        )
    ]
    win_load = pltpu.make_async_copy(win_hbm, win_ref, load_sem.at[0])
    wout_load = pltpu.make_async_copy(wout_hbm, wout_ref, load_sem.at[1])
    sec, me, head = lax.axis_index("section"), lax.axis_index("expert"), lax.axis_index("head")
    other = 1 - head
    upper = lax.div(2 * me, experts)
    micro, tok, half = local_ref.shape
    full = 2 * half
    total = experts * pad
    groups = total // tok
    piece_rows = total // SPLIT
    hidden_half = win_ref.shape[1]
    chunks = hidden_half // COLS
    own_cols = pl.ds(pl.multiple_of(head * half, 128), half)
    other_cols = pl.ds(pl.multiple_of(other * half, 128), half)

    barrier = pltpu.get_barrier_semaphore()

    def greet(k, carry):
        d = lax.rem(me + k, experts)
        for h in range(2):
            pl.semaphore_signal(
                barrier, inc=1, device_id={"expert": d, "head": h}, device_id_type=MESH
            )
        return carry

    lax.fori_loop(1, experts, greet, 0)
    pl.semaphore_signal(barrier, inc=1, device_id={"head": other}, device_id_type=MESH)
    pl.semaphore_signal(barrier, inc=1, device_id={"section": 1 - sec}, device_id_type=MESH)
    for load in small:
        load.start()
    win_load.start()
    wout_load.start()
    for load in small:
        load.wait()

    def far_first(k):
        return k * upper + (experts - 1 - k) * (1 - upper)

    def near_first(k):
        return far_first(experts - 1 - k)

    def each(order, action, with_me, lo=0, hi=experts):
        def step(k, carry):
            d = order(k)
            if with_me:
                action(d)
            else:
                pl.when(d != me)(lambda: action(d))
            return carry

        lax.fori_loop(lo, hi, step, 0)

    def slot_rows(index):
        return pl.ds(pl.multiple_of(index * pad, pad), pad)

    def micro_rows(m, index):
        return pl.ds(pl.multiple_of(m * total + index * pad, pad), pad)

    def span(m):
        return slice(m * total, (m + 1) * total)

    eye = lax.broadcasted_iota(jnp.int32, (tok, tok), 0) == lax.broadcasted_iota(
        jnp.int32, (tok, tok), 1
    )

    def to_col(row):
        return jnp.sum(jnp.where(eye, row, 0.0), axis=1, keepdims=True)

    def to_row(col):
        return jnp.sum(jnp.where(eye, col, 0.0), axis=0, keepdims=True)

    def fill_tab(ref, m, target):
        place_of = lax.broadcasted_iota(jnp.int32, (total, tok), 0).astype(F32)
        ref[m] = jnp.where(target == place_of, 1.0, 0.0).astype(BF16)

    for m in range(micro):
        ids, slots = ids_ref[m : m + 1, :], slots_ref[m : m + 1, :]
        target = jnp.where(slots < cap, ids * pad + slots, -1).astype(F32)
        fill_tab(tab, m, target)
        route[m : m + 1, :] = target
        route[micro + m : micro + m + 1, :] = prob_ref[m : m + 1, :]
    prob = [to_col(prob_ref[m : m + 1, :]) for m in range(micro)]
    gain = gain_ref[...]

    route_copy = pltpu.make_async_remote_copy(
        src_ref=route,
        dst_ref=route_in,
        send_sem=s8,
        recv_sem=r8,
        device_id={"section": 1 - sec},
        device_id_type=MESH,
    )

    def route_done():
        route_copy.wait_recv()
        for m in range(micro):
            fill_tab(tab2, m, route_in[m : m + 1, :])

    HOME, AWAY = 0, 1

    def target_section(slot):
        return sec if slot == HOME else 1 - sec

    def chunk_copy(slot, kind, m, dst, came_from):
        return pltpu.make_async_remote_copy(
            src_ref=send.at[slot, m, slot_rows(dst), :],
            dst_ref=rows.at[kind, micro_rows(m, came_from), own_cols],
            send_sem=s1.at[slot, m],
            recv_sem=r1.at[kind, m, came_from],
            device_id={"section": target_section(slot), "expert": dst},
            device_id_type=MESH,
        )

    def cross_copy(slot, kind, m, dst, came_from, cols):
        return pltpu.make_async_remote_copy(
            src_ref=send.at[slot, m, slot_rows(dst), :],
            dst_ref=rows.at[kind, micro_rows(m, came_from), cols],
            send_sem=s2.at[slot, m],
            recv_sem=r2.at[kind, m],
            device_id={"section": target_section(slot), "expert": dst, "head": other},
            device_id_type=MESH,
        )

    def relay_copy(kind, m, block, cols):
        return pltpu.make_async_remote_copy(
            src_ref=rows.at[kind, micro_rows(m, block), cols],
            dst_ref=rows.at[kind, micro_rows(m, block), cols],
            send_sem=s7.at[kind, m],
            recv_sem=r2.at[kind, m],
            device_id={"head": other},
            device_id_type=MESH,
        )

    def place(slot, m, tokens):
        table = tab if slot == HOME else tab2
        send[slot, m] = dot(table[m], tokens).astype(BF16)

    def dispatch(slot, kind, m, relay):
        def both_heads(d):
            chunk_copy(slot, kind, m, d, me).start()
            if not relay:
                cross_copy(slot, kind, m, d, me, own_cols).start()

        each(near_first if relay and RELAY_NEAR else far_first, both_heads, slot == AWAY)
        if slot == HOME:
            rows[kind, micro_rows(m, me), own_cols] = send[slot, m, slot_rows(me), :]
            if not relay:
                cross_copy(slot, kind, m, me, me, own_cols).start()

    def pump(slot, kind, m, relay):
        def one(block):
            chunk_copy(slot, kind, m, block, block).wait_recv()
            if relay:
                relay_copy(kind, m, block, own_cols).start()

        if slot == HOME and relay:
            relay_copy(kind, m, me, own_cols).start()
        each(near_first, one, slot == AWAY)

    def arrived(kind, m):
        relayed_blocks(kind, m, other_cols).wait_recv()

    def sent(slot, kind, m, relay):
        blocks = experts if slot == AWAY else experts - 1
        pltpu.make_async_remote_copy(
            src_ref=send.at[slot, m, 0 : blocks * pad, :],
            dst_ref=rows.at[kind, 0 : blocks * pad, own_cols],
            send_sem=s1.at[slot, m],
            recv_sem=r1.at[kind, m, 0],
            device_id={"head": other},
            device_id_type=MESH,
        ).wait_send()
        if not relay:
            pltpu.make_async_remote_copy(
                src_ref=send.at[slot, m],
                dst_ref=rows.at[kind, 0:total, own_cols],
                send_sem=s2.at[slot, m],
                recv_sem=r2.at[kind, m],
                device_id={"head": other},
                device_id_type=MESH,
            ).wait_send()

    def relayed_blocks(kind, m, cols):
        return pltpu.make_async_remote_copy(
            src_ref=rows.at[kind, span(m), cols],
            dst_ref=rows.at[kind, span(m), cols],
            send_sem=s7.at[kind, m],
            recv_sem=r2.at[kind, m],
            device_id={"head": other},
            device_id_type=MESH,
        )

    def relay_sent(kind, m):
        relayed_blocks(kind, m, own_cols).wait_send()

    def piece_at(c):
        p = c * upper + (SPLIT - 1 - c) * (1 - upper)
        return p, pl.ds(pl.multiple_of(p * piece_rows, piece_rows), piece_rows)

    def away_copy(kind, m, c):
        _, part = piece_at(c)
        return pltpu.make_async_remote_copy(
            src_ref=away.at[kind, m, part, :],
            dst_ref=recvp.at[kind, m, part, :],
            send_sem=s3.at[kind, m, c],
            recv_sem=r3.at[kind, m, c],
            device_id={"head": other},
            device_id_type=MESH,
        )

    def back_copy(kind, m, dst, came_from):
        return pltpu.make_async_remote_copy(
            src_ref=keep.at[kind, m, slot_rows(dst), :],
            dst_ref=back.at[kind, m, slot_rows(came_from), :],
            send_sem=s4.at[kind, m],
            recv_sem=r4.at[kind, m],
            device_id={"expert": dst},
            device_id_type=MESH,
        )

    def straight_copy(kind, m, dst, came_from):
        return pltpu.make_async_remote_copy(
            src_ref=away.at[kind, m, slot_rows(dst), :],
            dst_ref=recvp.at[kind, m, slot_rows(came_from), :],
            send_sem=s3.at[kind, m, 0],
            recv_sem=r3.at[kind, m, 0],
            device_id={"expert": dst, "head": other},
            device_id_type=MESH,
        )

    def straight_blocks(kind, m):
        return pltpu.make_async_remote_copy(
            src_ref=away.at[kind, m],
            dst_ref=recvp.at[kind, m],
            send_sem=s3.at[kind, m, 0],
            recv_sem=r3.at[kind, m, 0],
            device_id={"head": other},
            device_id_type=MESH,
        )

    def piece_blocks(c):
        return c * experts // SPLIT, (c + 1) * experts // SPLIT

    def send_straight(kind, m, lo, hi):
        each(far_first, lambda dst: straight_copy(kind, m, dst, me).start(), True, lo, hi)

    def send_same(kind, m, lo, hi):
        each(far_first, lambda dst: back_copy(kind, m, dst, me).start(), False, lo, hi)

    def keep_own(kind, m):
        back[kind, m, slot_rows(me), :] = keep[kind, m, slot_rows(me), :]

    def back_blocks(kind, m):
        return pltpu.make_async_remote_copy(
            src_ref=keep.at[kind, m, 0 : (experts - 1) * pad, :],
            dst_ref=back.at[kind, m, 0 : (experts - 1) * pad, :],
            send_sem=s4.at[kind, m],
            recv_sem=r4.at[kind, m],
            device_id={"head": other},
            device_id_type=MESH,
        )

    def send_back(kind, m):
        if kind == BWD:
            sum_copy(m).wait_recv()
        for c in range(SPLIT):
            p, part = piece_at(c)
            away_copy(kind, m, c).wait_recv()
            if kind == FWD:
                summed = keep[kind, m, part, :].astype(F32) + recvp[kind, m, part, :].astype(F32)
                keep[kind, m, part, :] = summed.astype(BF16)
            else:
                for i in range(groups // SPLIT):
                    g = p * (groups // SPLIT) + i
                    here = pl.ds(pl.multiple_of(g * tok, tok), tok)
                    there = pl.ds(pl.multiple_of(m * total + g * tok, tok), tok)
                    cross = to_col(xsend[m, pl.ds(g, 1), :] + xrecv[m, pl.ds(g, 1), :])
                    inv = inv_ref[there, :]
                    grad = keep[kind, m, here, :].astype(F32) + recvp[kind, m, here, :].astype(F32)
                    values = rows[FWD, there, own_cols].astype(F32)
                    delta = inv * (gain_ref[:, own_cols] * grad) - values * (
                        inv * inv * inv * cross / full
                    )
                    keep[kind, m, here, :] = delta.astype(BF16)
            send_same(kind, m, *piece_blocks(c))
        keep_own(kind, m)

    def collect(kind, m, straight):
        back_blocks(kind, m).wait_recv()
        found = dot(tab[m], back[kind, m], TN)
        if straight:
            straight_blocks(kind, m).wait_recv()
            found = found + dot(tab[m], recvp[kind, m], TN)
        return found

    def section_copy(m):
        return pltpu.make_async_remote_copy(
            src_ref=sec_src.at[m],
            dst_ref=sec_in.at[m],
            send_sem=s5.at[m],
            recv_sem=r5.at[m],
            device_id={"section": 1 - sec},
            device_id_type=MESH,
        )

    def sum_copy(m):
        return pltpu.make_async_remote_copy(
            src_ref=xsend.at[m],
            dst_ref=xrecv.at[m],
            send_sem=s6.at[m],
            recv_sem=r6.at[m],
            device_id={"head": other},
            device_id_type=MESH,
        )

    def normalize(m):
        values = rows[FWD, span(m), :].astype(F32)
        inv_scale = lax.rsqrt(jnp.mean(values * values, axis=-1, keepdims=True) + EPSILON)
        inv_ref[span(m), :] = inv_scale
        normed[span(m), :] = (values * inv_scale * gain).astype(BF16)

    def each_chunk(action):
        def step(c, carry):
            action(pl.ds(pl.multiple_of(c * COLS, COLS), COLS))
            return carry

        lax.fori_loop(0, chunks, step, 0, unroll=UNROLL if total <= 512 else 1)

    def out_partial(m, straight):
        away[FWD, m] = dot(act[span(m), :], wout_ref[:, other_cols]).astype(BF16)
        if straight:
            send_straight(FWD, m, 0, experts)
        else:
            for c in range(SPLIT):
                away_copy(FWD, m, c).start()
        keep[FWD, m] = dot(act[span(m), :], wout_ref[:, own_cols]).astype(BF16)
        if straight:
            send_same(FWD, m, 0, experts)
            keep_own(FWD, m)

    def grad_straight(m):
        away[BWD, m] = dot(gpre[span(m), :], win_ref[other_cols, :], NT).astype(BF16)
        keep[BWD, m] = dot(gpre[span(m), :], win_ref[own_cols, :], NT).astype(BF16)
        sides = ((away, other_cols), (keep, own_cols))
        for c in range(SPLIT):
            p, _ = piece_at(c)
            for i in range(groups // SPLIT):
                g = p * (groups // SPLIT) + i
                here = pl.ds(pl.multiple_of(g * tok, tok), tok)
                there = pl.ds(pl.multiple_of(m * total + g * tok, tok), tok)
                scaled = [ref[BWD, m, here, :].astype(F32) * gain_ref[:, cols] for ref, cols in sides]
                values = [rows[FWD, there, cols].astype(F32) for _, cols in sides]
                cross = jnp.sum(
                    scaled[0] * values[0] + scaled[1] * values[1], axis=1, keepdims=True
                )
                inv = inv_ref[there, :]
                cubed = inv * inv * inv * cross / full
                for (ref, _), part, value in zip(sides, scaled, values):
                    ref[BWD, m, here, :] = (inv * part - value * cubed).astype(BF16)
            send_straight(BWD, m, *piece_blocks(c))
            send_same(BWD, m, *piece_blocks(c))
        keep_own(BWD, m)

    def grad_partial(m, straight):
        if straight:
            grad_straight(m)
            return
        away[BWD, m] = dot(gpre[span(m), :], win_ref[other_cols, :], NT).astype(BF16)
        for c in range(SPLIT):
            away_copy(BWD, m, c).start()
        keep[BWD, m] = dot(gpre[span(m), :], win_ref[own_cols, :], NT).astype(BF16)
        for g in range(groups):
            here = slice(g * tok, (g + 1) * tok)
            there = slice(m * total + g * tok, m * total + (g + 1) * tok)
            cross = jnp.zeros((tok, 1), F32)
            for ref, cols in ((away, other_cols), (keep, own_cols)):
                scaled = ref[BWD, m, here, :].astype(F32) * gain_ref[:, cols]
                cross = cross + jnp.sum(
                    scaled * rows[FWD, there, cols].astype(F32), axis=1, keepdims=True
                )
            xsend[m, g : g + 1, :] = to_row(cross)
        sum_copy(m).start()

    def layer_out(m, tokens, straight):
        return (tokens.astype(F32) + prob[m] * collect(FWD, m, straight)).astype(BF16)

    def sent_grad(weight, cot):
        return (weight * cot.astype(F32)).astype(BF16)

    def layer_grad(m, cot, straight):
        return (cot.astype(F32) + collect(BWD, m, straight)).astype(BF16)

    def left(kind, m, straight):
        back_blocks(kind, m).wait_send()
        if straight:
            straight_blocks(kind, m).wait_send()
            return
        for c in range(SPLIT):
            away_copy(kind, m, c).wait_send()
        if kind == BWD:
            sum_copy(m).wait_send()

    def in_grads():
        def first(c, carry):
            part = pl.ds(pl.multiple_of(c * COLS, COLS), COLS)
            gin_ref[part, :] = dot(normed[:, part], gpre[...], TN).astype(BF16)
            return carry

        lax.fori_loop(0, full // COLS, first, 0, unroll=3 if total <= 512 else 1)

    def out_grads():
        def second(part):
            gout_ref[part, :] = dot(act[:, part], rows[BWD], TN).astype(BF16)

        each_chunk(second)

    @pl.when(sec == 0)
    def _():
        own_fwd, own_bwd, their_fwd = relayed["f0"], relayed["b0"], relayed["f1"]
        fwd_straight, bwd_straight = direct["f0"], direct["b0"]
        for m in range(micro):
            place(HOME, m, local_ref[m])
        pl.semaphore_wait(barrier, 2 * experts)
        dispatch(HOME, FWD, 0, own_fwd[0])
        if own_fwd[1]:
            dispatch(HOME, FWD, 1, own_fwd[1])
        route_copy.start()
        win_load.wait()
        wout_load.wait()
        pump(HOME, FWD, 0, own_fwd[0])

        def signal_turn():
            pl.semaphore_signal(turn, inc=1, device_id={"section": 1 - sec}, device_id_type=MESH)

        if TURN_AT == 0:
            signal_turn()
        if PUMP_AT == 0 and own_fwd[1]:
            pump(HOME, FWD, 1, own_fwd[1])

        def forward(m):
            arrived(FWD, m)
            if m == 0 and TURN_AT == 1:
                signal_turn()
            if m == 0 and not own_fwd[1]:
                dispatch(HOME, FWD, 1, own_fwd[1])
            normalize(m)

            def chunk(part):
                pre = dot(normed[span(m), :], win_ref[:, part])
                value, slope = activate(pre)
                act[span(m), part] = value.astype(BF16)
                mid[span(m), part] = slope.astype(mid.dtype)

            each_chunk(chunk)

        def hidden(m):
            sec_src[m] = layer_out(m, local_ref[m], fwd_straight[m])
            place(AWAY, m, sec_src[m])
            dispatch(AWAY, FWD, m, their_fwd[m])
            section_copy(m).start()

        forward(0)
        if PUMP_AT == 1 and own_fwd[1]:
            pump(HOME, FWD, 1, own_fwd[1])
        out_partial(0, fwd_straight[0])
        route_done()
        if not own_fwd[1]:
            pump(HOME, FWD, 1, own_fwd[1])
        forward(1)
        if not fwd_straight[0]:
            send_back(FWD, 0)
        if HOLD == 1:
            signal_turn()
        out_partial(1, fwd_straight[1])
        hidden(0)
        if HOLD == 2:
            signal_turn()
        if not fwd_straight[1]:
            send_back(FWD, 1)
        hidden(1)

        def backward(m):
            pump(AWAY, BWD, m, own_bwd[m])
            arrived(BWD, m)

            def chunk(part):
                grad_act = dot(rows[BWD, span(m), :], wout_ref[part, :], NT)
                gpre[span(m), part] = (grad_act * mid[span(m), part].astype(F32)).astype(BF16)

            each_chunk(chunk)

        backward(0)
        grad_partial(0, bwd_straight[0])
        backward(1)
        if not bwd_straight[0]:
            send_back(BWD, 0)
        grad_partial(1, bwd_straight[1])
        out_grads()
        if not bwd_straight[1]:
            send_back(BWD, 1)
        section_copy(0).wait_recv()
        out_ref[0] = layer_grad(0, sec_in[0], bwd_straight[0])
        in_grads()
        section_copy(1).wait_recv()
        out_ref[1] = layer_grad(1, sec_in[1], bwd_straight[1])

        for m in range(micro):
            left(FWD, m, fwd_straight[m])
            left(BWD, m, bwd_straight[m])
            sent(HOME, FWD, m, own_fwd[m])
            sent(AWAY, FWD, m, their_fwd[m])
            if own_fwd[m]:
                relay_sent(FWD, m)
            if own_bwd[m]:
                relay_sent(BWD, m)

    @pl.when(sec != 0)
    def _():
        own_bwd, own_fwd, their_bwd = relayed["b1"], relayed["f1"], relayed["b0"]
        fwd_straight, bwd_straight = direct["f1"], direct["b1"]
        for m in range(micro):
            place(HOME, m, sent_grad(prob[m], local_ref[m]))
        pl.semaphore_wait(barrier, 2 * experts)
        route_copy.start()
        win_load.wait()
        wout_load.wait()

        pl.semaphore_wait(turn, 1)
        for m in range(micro):
            dispatch(HOME, BWD, m, own_bwd[m])
        if HOLD:
            pl.semaphore_wait(turn, 1)
        for m in range(micro):
            pump(HOME, BWD, m, own_bwd[m])

        def early_grad(m):
            arrived(BWD, m)

            def early(part):
                grad_act = dot(rows[BWD, span(m), :], wout_ref[part, :], NT)
                mid[span(m), part] = grad_act.astype(mid.dtype)

            each_chunk(early)

        early_grad(0)
        route_done()
        prob_in = [to_col(route_in[micro + m : micro + m + 1, :]) for m in range(micro)]
        early_grad(1)

        def both(m):
            arrived(FWD, m)
            normalize(m)

            def chunk(part):
                pre = dot(normed[span(m), :], win_ref[:, part])
                value, slope = activate(pre)
                act[span(m), part] = value.astype(BF16)
                gpre[span(m), part] = (mid[span(m), part].astype(F32) * slope).astype(BF16)

            each_chunk(chunk)

        def finish(m):
            sec_src[m] = layer_grad(m, local_ref[m], bwd_straight[m])
            place(AWAY, m, sent_grad(prob_in[m], sec_src[m]))
            dispatch(AWAY, BWD, m, their_bwd[m])
            section_copy(m).start()

        pump(AWAY, FWD, 0, own_fwd[0])
        both(0)
        grad_partial(0, bwd_straight[0])
        if not bwd_straight[0]:
            send_back(BWD, 0)
        if ORDER == 1:
            finish(0)
        pump(AWAY, FWD, 1, own_fwd[1])
        both(1)
        if ORDER == 2:
            finish(0)
        grad_partial(1, bwd_straight[1])
        if ORDER == 3:
            finish(0)
        if not bwd_straight[1]:
            send_back(BWD, 1)
        if TAIL == 0:
            out_partial(0, fwd_straight[0])
            out_partial(1, fwd_straight[1])
        finish(1)
        if TAIL == 1:
            out_partial(0, fwd_straight[0])
            out_partial(1, fwd_straight[1])
        in_grads()
        if TAIL == 2:
            out_partial(0, fwd_straight[0])
            out_partial(1, fwd_straight[1])
        out_grads()
        if TAIL == 3:
            out_partial(0, fwd_straight[0])
            out_partial(1, fwd_straight[1])
        if not fwd_straight[0]:
            send_back(FWD, 0)
        if not fwd_straight[1]:
            send_back(FWD, 1)
        for m in range(micro):
            section_copy(m).wait_recv()
            out_ref[m] = layer_out(m, sec_in[m], fwd_straight[m])

        for m in range(micro):
            left(FWD, m, fwd_straight[m])
            left(BWD, m, bwd_straight[m])
            sent(HOME, BWD, m, own_bwd[m])
            sent(AWAY, BWD, m, their_bwd[m])
            if own_fwd[m]:
                relay_sent(FWD, m)
            if own_bwd[m]:
                relay_sent(BWD, m)

    for m in range(micro):
        section_copy(m).wait_send()
    route_copy.wait_send()


def copy_out(out_in, gin_in, gout_in, out_ref, gin_ref, gout_ref, sem):
    pairs = ((gin_in, gin_ref), (gout_in, gout_ref), (out_in, out_ref))
    copies = [pltpu.make_async_copy(a, b, sem.at[i]) for i, (a, b) in enumerate(pairs)]
    for copy in copies:
        copy.start()
    for copy in copies:
        copy.wait()


def on_device(boundary, norm_gain, gate_prob, expert_ids, slot_ids, weight_in, weight_out):
    experts = lax.axis_size("expert")
    micro, tok, half = boundary.shape[1:]
    full, hidden_half = weight_in.shape[2:]
    cap = 2 * tok // experts
    pad = -(-cap // 16) * 16
    total = experts * pad
    mid_type = F32 if total <= 512 else BF16
    vmem = pl.BlockSpec(memory_space=pltpu.VMEM)
    anywhere = pl.BlockSpec(memory_space=pl.ANY)
    per_block = pltpu.SemaphoreType.DMA((2, micro, experts))
    per_pair = pltpu.SemaphoreType.DMA((2, micro))
    per_piece = pltpu.SemaphoreType.DMA((2, micro, SPLIT))
    per_micro = pltpu.SemaphoreType.DMA((micro,))
    pieces = pltpu.VMEM((2, micro, total, half), BF16)
    tokens = pltpu.VMEM((micro, tok, half), BF16)
    sums = pltpu.VMEM((micro, max(8, total // tok), tok), F32)
    routes = pltpu.VMEM((8, tok), F32)
    table = pltpu.VMEM((micro, total, tok), BF16)
    out, grad_in, grad_out = pl.pallas_call(
        functools.partial(kernel, experts, cap, pad, RELAYED, DIRECT),
        out_shape=(
            pltpu.VMEM((micro, tok, half), BF16),
            pltpu.VMEM((full, hidden_half), BF16),
            pltpu.VMEM((hidden_half, full), BF16),
        ),
        in_specs=[anywhere] * 7,
        out_specs=(vmem, vmem, vmem),
        scratch_shapes=[
            table,
            table,
            pieces,
            pltpu.VMEM((2, micro * total, full), BF16),
            pltpu.VMEM((micro * total, full), BF16),
            pltpu.VMEM((micro * total, hidden_half), BF16),
            pltpu.VMEM((micro * total, hidden_half), BF16),
            pltpu.VMEM((micro * total, hidden_half), mid_type),
            pltpu.VMEM((micro * total, 1), F32),
            pieces,
            pieces,
            pieces,
            pieces,
            tokens,
            tokens,
            sums,
            sums,
            routes,
            routes,
            pltpu.VMEM((full, hidden_half), BF16),
            pltpu.VMEM((hidden_half, full), BF16),
            tokens,
            pltpu.VMEM((1, full), F32),
            pltpu.VMEM((micro, tok), F32),
            pltpu.VMEM((micro, tok), jnp.int32),
            pltpu.VMEM((micro, tok), jnp.int32),
            pltpu.SemaphoreType.DMA((7,)),
            pltpu.SemaphoreType.REGULAR,
            per_pair, per_block,
            per_pair, per_pair,
            per_piece, per_piece,
            per_pair, per_pair,
            per_micro, per_micro,
            per_micro, per_micro,
            per_pair,
            pltpu.SemaphoreType.DMA,
            pltpu.SemaphoreType.DMA,
        ],
        compiler_params=pltpu.CompilerParams(
            collective_id=0, has_side_effects=True, vmem_limit_bytes=VMEM_LIMIT
        ),
    )(
        boundary[0], norm_gain, gate_prob[0], expert_ids[0], slot_ids[0],
        weight_in[0, 0], weight_out[0, 0],
    )
    results = (out, grad_in, grad_out)
    out, grad_in, grad_out = pl.pallas_call(
        copy_out,
        out_shape=[jax.ShapeDtypeStruct(x.shape, x.dtype) for x in results],
        in_specs=[vmem] * 3,
        out_specs=[anywhere] * 3,
        scratch_shapes=[pltpu.SemaphoreType.DMA((3,))],
        compiler_params=pltpu.CompilerParams(vmem_limit_bytes=COPY_LIMIT),
    )(*results)
    return (out[None], grad_in[None, None], grad_out[None, None])


def solution(mesh):
    placed = (
        P("section", None, "expert", "head"),
        P("section", None),
        P("section", None, "expert"),
        P("section", None, "expert"),
        P("section", None, "expert"),
        P("section", "expert", None, "head"),
        P("section", "expert", "head", None),
    )
    return jax.shard_map(
        on_device,
        mesh=mesh,
        in_specs=placed,
        out_specs=(
            P("section", None, "expert", "head"),
            P("section", "expert", None, "head"),
            P("section", "expert", "head", None),
        ),
        check_vma=False,
    )
```

```python
import functools

import jax
import jax.numpy as jnp
from jax import lax
from jax.experimental import pallas as pl
from jax.experimental.pallas import tpu as pltpu
from jax.sharding import PartitionSpec as P

EPSILON = 1e-06
ROOT_COEF = 0.7978845608
CUBE_COEF = 0.044715
MESH = pl.DeviceIdType.MESH
BF16 = jnp.bfloat16
F32 = jnp.float32
FWD, BWD = 0, 1
COLS = 256
SPLIT = 2
VMEM_LIMIT = 56 * 2**20
COPY_LIMIT = 2**20
RELAYED = {"f0": (True, True), "b1": (True, True), "f1": (True, False), "b0": (True, False)}
DIRECT = {"f0": (True, True), "b1": (True, False), "f1": (False, False), "b0": (False, True)}
RELAY_NEAR = True
TURN_AT = 0
HOLD = 1
TAIL = 7
PARTS = (1, 1, 1)
ORDER = 3
UNROLL = 6
PUMP_AT = 0


def activate(pre_act):
    tangent = jnp.tanh(ROOT_COEF * (pre_act + CUBE_COEF * pre_act * pre_act * pre_act))
    act_value = 0.5 * pre_act * (1.0 + tangent)
    act_slope = 0.5 * (1.0 + tangent) + 0.5 * pre_act * (1.0 - tangent * tangent) * ROOT_COEF * (
        1.0 + 3.0 * CUBE_COEF * pre_act * pre_act
    )
    return (act_value, act_slope)


def dot(left, right, dims=((1,), (0,))):
    return lax.dot_general(left, right, (dims, ((), ())), preferred_element_type=F32)


NT = ((1,), (1,))
TN = ((0,), (0,))


def kernel(
    experts, cap, pad, relayed, direct,
    local_hbm, gain_hbm, prob_hbm, ids_hbm, slots_hbm, win_hbm, wout_hbm,
    out_ref, gin_ref, gout_ref,
    tab, tab2, send, rows, normed, act, gpre, mid, inv_ref, keep, away, recvp, back,
    sec_src, sec_in, xsend, xrecv, route, route_in, win_ref, wout_ref,
    local_ref, gain_ref, prob_ref, ids_ref, slots_ref, load_sem, turn,
    s1, r1, s2, r2, s3, r3, s4, r4, s5, r5, s6, r6, s7, s8, r8,
):
    small = [
        pltpu.make_async_copy(source, target, load_sem.at[2 + i])
        for i, (source, target) in enumerate(
            (
                (local_hbm, local_ref),
                (gain_hbm, gain_ref),
                (prob_hbm, prob_ref),
                (ids_hbm, ids_ref),
                (slots_hbm, slots_ref),
            )
        )
    ]
    win_load = pltpu.make_async_copy(win_hbm, win_ref, load_sem.at[0])
    wout_load = pltpu.make_async_copy(wout_hbm, wout_ref, load_sem.at[1])
    sec, me, head = lax.axis_index("section"), lax.axis_index("expert"), lax.axis_index("head")
    other = 1 - head
    upper = lax.div(2 * me, experts)
    micro, tok, half = local_ref.shape
    full = 2 * half
    total = experts * pad
    groups = total // tok
    piece_rows = total // SPLIT
    hidden_half = win_ref.shape[1]
    chunks = hidden_half // COLS
    own_cols = pl.ds(pl.multiple_of(head * half, 128), half)
    other_cols = pl.ds(pl.multiple_of(other * half, 128), half)

    barrier = pltpu.get_barrier_semaphore()

    def greet(k, carry):
        d = lax.rem(me + k, experts)
        for h in range(2):
            pl.semaphore_signal(
                barrier, inc=1, device_id={"expert": d, "head": h}, device_id_type=MESH
            )
        return carry

    lax.fori_loop(1, experts, greet, 0)
    pl.semaphore_signal(barrier, inc=1, device_id={"head": other}, device_id_type=MESH)
    pl.semaphore_signal(barrier, inc=1, device_id={"section": 1 - sec}, device_id_type=MESH)
    for load in small:
        load.start()
    win_load.start()
    wout_load.start()
    for load in small:
        load.wait()

    def far_first(k):
        return k * upper + (experts - 1 - k) * (1 - upper)

    def near_first(k):
        return far_first(experts - 1 - k)

    def each(order, action, with_me, lo=0, hi=experts):
        def step(k, carry):
            d = order(k)
            if with_me:
                action(d)
            else:
                pl.when(d != me)(lambda: action(d))
            return carry

        lax.fori_loop(lo, hi, step, 0)

    def slot_rows(index):
        return pl.ds(pl.multiple_of(index * pad, pad), pad)

    def micro_rows(m, index):
        return pl.ds(pl.multiple_of(m * total + index * pad, pad), pad)

    def span(m):
        return slice(m * total, (m + 1) * total)

    eye = lax.broadcasted_iota(jnp.int32, (tok, tok), 0) == lax.broadcasted_iota(
        jnp.int32, (tok, tok), 1
    )

    def to_col(row):
        return jnp.sum(jnp.where(eye, row, 0.0), axis=1, keepdims=True)

    def to_row(col):
        return jnp.sum(jnp.where(eye, col, 0.0), axis=0, keepdims=True)

    def fill_tab(ref, m, target):
        place_of = lax.broadcasted_iota(jnp.int32, (total, tok), 0).astype(F32)
        ref[m] = jnp.where(target == place_of, 1.0, 0.0).astype(BF16)

    for m in range(micro):
        ids, slots = ids_ref[m : m + 1, :], slots_ref[m : m + 1, :]
        target = jnp.where(slots < cap, ids * pad + slots, -1).astype(F32)
        fill_tab(tab, m, target)
        route[m : m + 1, :] = target
        route[micro + m : micro + m + 1, :] = prob_ref[m : m + 1, :]
    prob = [to_col(prob_ref[m : m + 1, :]) for m in range(micro)]
    gain = gain_ref[...]

    route_copy = pltpu.make_async_remote_copy(
        src_ref=route,
        dst_ref=route_in,
        send_sem=s8,
        recv_sem=r8,
        device_id={"section": 1 - sec},
        device_id_type=MESH,
    )

    def route_done():
        route_copy.wait_recv()
        for m in range(micro):
            fill_tab(tab2, m, route_in[m : m + 1, :])

    HOME, AWAY = 0, 1

    def target_section(slot):
        return sec if slot == HOME else 1 - sec

    def chunk_copy(slot, kind, m, dst, came_from):
        return pltpu.make_async_remote_copy(
            src_ref=send.at[slot, m, slot_rows(dst), :],
            dst_ref=rows.at[kind, micro_rows(m, came_from), own_cols],
            send_sem=s1.at[slot, m],
            recv_sem=r1.at[kind, m, came_from],
            device_id={"section": target_section(slot), "expert": dst},
            device_id_type=MESH,
        )

    def cross_copy(slot, kind, m, dst, came_from, cols):
        return pltpu.make_async_remote_copy(
            src_ref=send.at[slot, m, slot_rows(dst), :],
            dst_ref=rows.at[kind, micro_rows(m, came_from), cols],
            send_sem=s2.at[slot, m],
            recv_sem=r2.at[kind, m],
            device_id={"section": target_section(slot), "expert": dst, "head": other},
            device_id_type=MESH,
        )

    def relay_copy(kind, m, block, cols):
        return pltpu.make_async_remote_copy(
            src_ref=rows.at[kind, micro_rows(m, block), cols],
            dst_ref=rows.at[kind, micro_rows(m, block), cols],
            send_sem=s7.at[kind, m],
            recv_sem=r2.at[kind, m],
            device_id={"head": other},
            device_id_type=MESH,
        )

    def place(slot, m, tokens):
        table = tab if slot == HOME else tab2
        send[slot, m] = dot(table[m], tokens).astype(BF16)

    def dispatch(slot, kind, m, relay):
        def both_heads(d):
            chunk_copy(slot, kind, m, d, me).start()
            if not relay:
                cross_copy(slot, kind, m, d, me, own_cols).start()

        each(near_first if relay and RELAY_NEAR else far_first, both_heads, slot == AWAY)
        if slot == HOME:
            rows[kind, micro_rows(m, me), own_cols] = send[slot, m, slot_rows(me), :]
            if not relay:
                cross_copy(slot, kind, m, me, me, own_cols).start()

    def pump(slot, kind, m, relay):
        def one(block):
            chunk_copy(slot, kind, m, block, block).wait_recv()
            if relay:
                relay_copy(kind, m, block, own_cols).start()

        if slot == HOME and relay:
            relay_copy(kind, m, me, own_cols).start()
        each(near_first, one, slot == AWAY)

    def arrived(kind, m):
        relayed_blocks(kind, m, other_cols).wait_recv()

    def sent(slot, kind, m, relay):
        blocks = experts if slot == AWAY else experts - 1
        pltpu.make_async_remote_copy(
            src_ref=send.at[slot, m, 0 : blocks * pad, :],
            dst_ref=rows.at[kind, 0 : blocks * pad, own_cols],
            send_sem=s1.at[slot, m],
            recv_sem=r1.at[kind, m, 0],
            device_id={"head": other},
            device_id_type=MESH,
        ).wait_send()
        if not relay:
            pltpu.make_async_remote_copy(
                src_ref=send.at[slot, m],
                dst_ref=rows.at[kind, 0:total, own_cols],
                send_sem=s2.at[slot, m],
                recv_sem=r2.at[kind, m],
                device_id={"head": other},
                device_id_type=MESH,
            ).wait_send()

    def relayed_blocks(kind, m, cols):
        return pltpu.make_async_remote_copy(
            src_ref=rows.at[kind, span(m), cols],
            dst_ref=rows.at[kind, span(m), cols],
            send_sem=s7.at[kind, m],
            recv_sem=r2.at[kind, m],
            device_id={"head": other},
            device_id_type=MESH,
        )

    def relay_sent(kind, m):
        relayed_blocks(kind, m, own_cols).wait_send()

    def piece_at(c):
        p = c * upper + (SPLIT - 1 - c) * (1 - upper)
        return p, pl.ds(pl.multiple_of(p * piece_rows, piece_rows), piece_rows)

    def away_copy(kind, m, c):
        _, part = piece_at(c)
        return pltpu.make_async_remote_copy(
            src_ref=away.at[kind, m, part, :],
            dst_ref=recvp.at[kind, m, part, :],
            send_sem=s3.at[kind, m, c],
            recv_sem=r3.at[kind, m, c],
            device_id={"head": other},
            device_id_type=MESH,
        )

    def back_copy(kind, m, dst, came_from):
        return pltpu.make_async_remote_copy(
            src_ref=keep.at[kind, m, slot_rows(dst), :],
            dst_ref=back.at[kind, m, slot_rows(came_from), :],
            send_sem=s4.at[kind, m],
            recv_sem=r4.at[kind, m],
            device_id={"expert": dst},
            device_id_type=MESH,
        )

    def straight_copy(kind, m, dst, came_from):
        return pltpu.make_async_remote_copy(
            src_ref=away.at[kind, m, slot_rows(dst), :],
            dst_ref=recvp.at[kind, m, slot_rows(came_from), :],
            send_sem=s3.at[kind, m, 0],
            recv_sem=r3.at[kind, m, 0],
            device_id={"expert": dst, "head": other},
            device_id_type=MESH,
        )

    def straight_blocks(kind, m):
        return pltpu.make_async_remote_copy(
            src_ref=away.at[kind, m],
            dst_ref=recvp.at[kind, m],
            send_sem=s3.at[kind, m, 0],
            recv_sem=r3.at[kind, m, 0],
            device_id={"head": other},
            device_id_type=MESH,
        )

    def piece_blocks(c):
        return c * experts // SPLIT, (c + 1) * experts // SPLIT

    def send_straight(kind, m, lo, hi):
        each(far_first, lambda dst: straight_copy(kind, m, dst, me).start(), True, lo, hi)

    def send_same(kind, m, lo, hi):
        each(far_first, lambda dst: back_copy(kind, m, dst, me).start(), False, lo, hi)

    def keep_own(kind, m):
        back[kind, m, slot_rows(me), :] = keep[kind, m, slot_rows(me), :]

    def back_blocks(kind, m):
        return pltpu.make_async_remote_copy(
            src_ref=keep.at[kind, m, 0 : (experts - 1) * pad, :],
            dst_ref=back.at[kind, m, 0 : (experts - 1) * pad, :],
            send_sem=s4.at[kind, m],
            recv_sem=r4.at[kind, m],
            device_id={"head": other},
            device_id_type=MESH,
        )

    def send_back(kind, m):
        if kind == BWD:
            sum_copy(m).wait_recv()
        for c in range(SPLIT):
            p, part = piece_at(c)
            away_copy(kind, m, c).wait_recv()
            if kind == FWD:
                summed = keep[kind, m, part, :].astype(F32) + recvp[kind, m, part, :].astype(F32)
                keep[kind, m, part, :] = summed.astype(BF16)
            else:
                for i in range(groups // SPLIT):
                    g = p * (groups // SPLIT) + i
                    here = pl.ds(pl.multiple_of(g * tok, tok), tok)
                    there = pl.ds(pl.multiple_of(m * total + g * tok, tok), tok)
                    cross = to_col(xsend[m, pl.ds(g, 1), :] + xrecv[m, pl.ds(g, 1), :])
                    inv = inv_ref[there, :]
                    grad = keep[kind, m, here, :].astype(F32) + recvp[kind, m, here, :].astype(F32)
                    values = rows[FWD, there, own_cols].astype(F32)
                    delta = inv * (gain_ref[:, own_cols] * grad) - values * (
                        inv * inv * inv * cross / full
                    )
                    keep[kind, m, here, :] = delta.astype(BF16)
            send_same(kind, m, *piece_blocks(c))
        keep_own(kind, m)

    def collect(kind, m, straight):
        back_blocks(kind, m).wait_recv()
        found = dot(tab[m], back[kind, m], TN)
        if straight:
            straight_blocks(kind, m).wait_recv()
            found = found + dot(tab[m], recvp[kind, m], TN)
        return found

    def section_copy(m):
        return pltpu.make_async_remote_copy(
            src_ref=sec_src.at[m],
            dst_ref=sec_in.at[m],
            send_sem=s5.at[m],
            recv_sem=r5.at[m],
            device_id={"section": 1 - sec},
            device_id_type=MESH,
        )

    def sum_copy(m):
        return pltpu.make_async_remote_copy(
            src_ref=xsend.at[m],
            dst_ref=xrecv.at[m],
            send_sem=s6.at[m],
            recv_sem=r6.at[m],
            device_id={"head": other},
            device_id_type=MESH,
        )

    def normalize(m):
        values = rows[FWD, span(m), :].astype(F32)
        inv_scale = lax.rsqrt(jnp.mean(values * values, axis=-1, keepdims=True) + EPSILON)
        inv_ref[span(m), :] = inv_scale
        normed[span(m), :] = (values * inv_scale * gain).astype(BF16)

    def each_chunk(action):
        def step(c, carry):
            action(pl.ds(pl.multiple_of(c * COLS, COLS), COLS))
            return carry

        lax.fori_loop(0, chunks, step, 0, unroll=UNROLL if total <= 512 else 1)

    def out_partial(m, straight):
        away[FWD, m] = dot(act[span(m), :], wout_ref[:, other_cols]).astype(BF16)
        if straight:
            send_straight(FWD, m, 0, experts)
        else:
            for c in range(SPLIT):
                away_copy(FWD, m, c).start()
        keep[FWD, m] = dot(act[span(m), :], wout_ref[:, own_cols]).astype(BF16)
        if straight:
            send_same(FWD, m, 0, experts)
            keep_own(FWD, m)

    def grad_straight(m):
        away[BWD, m] = dot(gpre[span(m), :], win_ref[other_cols, :], NT).astype(BF16)
        keep[BWD, m] = dot(gpre[span(m), :], win_ref[own_cols, :], NT).astype(BF16)
        sides = ((away, other_cols), (keep, own_cols))
        for c in range(SPLIT):
            p, _ = piece_at(c)
            for i in range(groups // SPLIT):
                g = p * (groups // SPLIT) + i
                here = pl.ds(pl.multiple_of(g * tok, tok), tok)
                there = pl.ds(pl.multiple_of(m * total + g * tok, tok), tok)
                scaled = [ref[BWD, m, here, :].astype(F32) * gain_ref[:, cols] for ref, cols in sides]
                values = [rows[FWD, there, cols].astype(F32) for _, cols in sides]
                cross = jnp.sum(
                    scaled[0] * values[0] + scaled[1] * values[1], axis=1, keepdims=True
                )
                inv = inv_ref[there, :]
                cubed = inv * inv * inv * cross / full
                for (ref, _), part, value in zip(sides, scaled, values):
                    ref[BWD, m, here, :] = (inv * part - value * cubed).astype(BF16)
            send_straight(BWD, m, *piece_blocks(c))
            send_same(BWD, m, *piece_blocks(c))
        keep_own(BWD, m)

    def grad_partial(m, straight):
        if straight:
            grad_straight(m)
            return
        away[BWD, m] = dot(gpre[span(m), :], win_ref[other_cols, :], NT).astype(BF16)
        for c in range(SPLIT):
            away_copy(BWD, m, c).start()
        keep[BWD, m] = dot(gpre[span(m), :], win_ref[own_cols, :], NT).astype(BF16)
        for g in range(groups):
            here = slice(g * tok, (g + 1) * tok)
            there = slice(m * total + g * tok, m * total + (g + 1) * tok)
            cross = jnp.zeros((tok, 1), F32)
            for ref, cols in ((away, other_cols), (keep, own_cols)):
                scaled = ref[BWD, m, here, :].astype(F32) * gain_ref[:, cols]
                cross = cross + jnp.sum(
                    scaled * rows[FWD, there, cols].astype(F32), axis=1, keepdims=True
                )
            xsend[m, g : g + 1, :] = to_row(cross)
        sum_copy(m).start()

    def layer_out(m, tokens, straight):
        return (tokens.astype(F32) + prob[m] * collect(FWD, m, straight)).astype(BF16)

    def sent_grad(weight, cot):
        return (weight * cot.astype(F32)).astype(BF16)

    def layer_grad(m, cot, straight):
        return (cot.astype(F32) + collect(BWD, m, straight)).astype(BF16)

    def left(kind, m, straight):
        back_blocks(kind, m).wait_send()
        if straight:
            straight_blocks(kind, m).wait_send()
            return
        for c in range(SPLIT):
            away_copy(kind, m, c).wait_send()
        if kind == BWD:
            sum_copy(m).wait_send()

    def in_grads():
        def first(c, carry):
            part = pl.ds(pl.multiple_of(c * COLS, COLS), COLS)
            gin_ref[part, :] = dot(normed[:, part], gpre[...], TN).astype(BF16)
            return carry

        lax.fori_loop(0, full // COLS, first, 0, unroll=3 if total <= 512 else 1)

    def out_grads():
        def second(part):
            gout_ref[part, :] = dot(act[:, part], rows[BWD], TN).astype(BF16)

        each_chunk(second)

    @pl.when(sec == 0)
    def _():
        own_fwd, own_bwd, their_fwd = relayed["f0"], relayed["b0"], relayed["f1"]
        fwd_straight, bwd_straight = direct["f0"], direct["b0"]
        for m in range(micro):
            place(HOME, m, local_ref[m])
        pl.semaphore_wait(barrier, 2 * experts)
        dispatch(HOME, FWD, 0, own_fwd[0])
        if own_fwd[1]:
            dispatch(HOME, FWD, 1, own_fwd[1])
        route_copy.start()
        win_load.wait()
        wout_load.wait()
        pump(HOME, FWD, 0, own_fwd[0])

        def signal_turn():
            pl.semaphore_signal(turn, inc=1, device_id={"section": 1 - sec}, device_id_type=MESH)

        if TURN_AT == 0:
            signal_turn()
        if PUMP_AT == 0 and own_fwd[1]:
            pump(HOME, FWD, 1, own_fwd[1])

        def forward(m):
            arrived(FWD, m)
            if m == 0 and TURN_AT == 1:
                signal_turn()
            if m == 0 and not own_fwd[1]:
                dispatch(HOME, FWD, 1, own_fwd[1])
            normalize(m)

            def chunk(part):
                pre = dot(normed[span(m), :], win_ref[:, part])
                value, slope = activate(pre)
                act[span(m), part] = value.astype(BF16)
                mid[span(m), part] = slope.astype(mid.dtype)

            each_chunk(chunk)

        def hidden(m):
            sec_src[m] = layer_out(m, local_ref[m], fwd_straight[m])
            place(AWAY, m, sec_src[m])
            dispatch(AWAY, FWD, m, their_fwd[m])
            section_copy(m).start()

        forward(0)
        if PUMP_AT == 1 and own_fwd[1]:
            pump(HOME, FWD, 1, own_fwd[1])
        out_partial(0, fwd_straight[0])
        route_done()
        if not own_fwd[1]:
            pump(HOME, FWD, 1, own_fwd[1])
        forward(1)
        if not fwd_straight[0]:
            send_back(FWD, 0)
        if HOLD == 1:
            signal_turn()
        out_partial(1, fwd_straight[1])
        hidden(0)
        if HOLD == 2:
            signal_turn()
        if not fwd_straight[1]:
            send_back(FWD, 1)
        hidden(1)

        def backward(m):
            pump(AWAY, BWD, m, own_bwd[m])
            arrived(BWD, m)

            def chunk(part):
                grad_act = dot(rows[BWD, span(m), :], wout_ref[part, :], NT)
                gpre[span(m), part] = (grad_act * mid[span(m), part].astype(F32)).astype(BF16)

            each_chunk(chunk)

        backward(0)
        grad_partial(0, bwd_straight[0])
        backward(1)
        if not bwd_straight[0]:
            send_back(BWD, 0)
        grad_partial(1, bwd_straight[1])
        out_grads()
        if not bwd_straight[1]:
            send_back(BWD, 1)
        section_copy(0).wait_recv()
        out_ref[0] = layer_grad(0, sec_in[0], bwd_straight[0])
        in_grads()
        section_copy(1).wait_recv()
        out_ref[1] = layer_grad(1, sec_in[1], bwd_straight[1])

        for m in range(micro):
            left(FWD, m, fwd_straight[m])
            left(BWD, m, bwd_straight[m])
            sent(HOME, FWD, m, own_fwd[m])
            sent(AWAY, FWD, m, their_fwd[m])
            if own_fwd[m]:
                relay_sent(FWD, m)
            if own_bwd[m]:
                relay_sent(BWD, m)

    @pl.when(sec != 0)
    def _():
        own_bwd, own_fwd, their_bwd = relayed["b1"], relayed["f1"], relayed["b0"]
        fwd_straight, bwd_straight = direct["f1"], direct["b1"]
        for m in range(micro):
            place(HOME, m, sent_grad(prob[m], local_ref[m]))
        pl.semaphore_wait(barrier, 2 * experts)
        route_copy.start()
        win_load.wait()
        wout_load.wait()

        pl.semaphore_wait(turn, 1)
        for m in range(micro):
            dispatch(HOME, BWD, m, own_bwd[m])
        if HOLD:
            pl.semaphore_wait(turn, 1)
        for m in range(micro):
            pump(HOME, BWD, m, own_bwd[m])

        def early_grad(m):
            arrived(BWD, m)

            def early(part):
                grad_act = dot(rows[BWD, span(m), :], wout_ref[part, :], NT)
                mid[span(m), part] = grad_act.astype(mid.dtype)

            each_chunk(early)

        early_grad(0)
        route_done()
        prob_in = [to_col(route_in[micro + m : micro + m + 1, :]) for m in range(micro)]
        early_grad(1)

        def both(m):
            arrived(FWD, m)
            normalize(m)

            def chunk(part):
                pre = dot(normed[span(m), :], win_ref[:, part])
                value, slope = activate(pre)
                act[span(m), part] = value.astype(BF16)
                gpre[span(m), part] = (mid[span(m), part].astype(F32) * slope).astype(BF16)

            each_chunk(chunk)

        def finish(m):
            sec_src[m] = layer_grad(m, local_ref[m], bwd_straight[m])
            place(AWAY, m, sent_grad(prob_in[m], sec_src[m]))
            dispatch(AWAY, BWD, m, their_bwd[m])
            section_copy(m).start()

        pump(AWAY, FWD, 0, own_fwd[0])
        both(0)
        grad_partial(0, bwd_straight[0])
        if not bwd_straight[0]:
            send_back(BWD, 0)
        if ORDER == 1:
            finish(0)
        pump(AWAY, FWD, 1, own_fwd[1])
        both(1)
        if ORDER == 2:
            finish(0)
        grad_partial(1, bwd_straight[1])
        if TAIL == 5 or TAIL == 6:
            out_partial(0, fwd_straight[0])
            out_partial(1, fwd_straight[1])
        if TAIL == 7:
            out_partial(0, fwd_straight[0])
        if ORDER == 3:
            finish(0)
        if not bwd_straight[1]:
            send_back(BWD, 1)
        if TAIL == 7:
            out_partial(1, fwd_straight[1])
        if TAIL == 6:
            in_grads()
        if TAIL == 0:
            out_partial(0, fwd_straight[0])
            out_partial(1, fwd_straight[1])
        if TAIL == 8:
            out_partial(0, fwd_straight[0])
        finish(1)
        if TAIL == 8:
            in_grads()
            out_grads()
            out_partial(1, fwd_straight[1])
        if TAIL == 1:
            out_partial(0, fwd_straight[0])
            out_partial(1, fwd_straight[1])
        if TAIL != 6 and TAIL != 8:
            in_grads()
        if TAIL == 2:
            out_partial(0, fwd_straight[0])
            out_partial(1, fwd_straight[1])
        if TAIL != 8:
            out_grads()
        if TAIL == 3:
            out_partial(0, fwd_straight[0])
            out_partial(1, fwd_straight[1])
        if not fwd_straight[0]:
            send_back(FWD, 0)
        if not fwd_straight[1]:
            send_back(FWD, 1)
        for m in range(micro):
            section_copy(m).wait_recv()
            out_ref[m] = layer_out(m, sec_in[m], fwd_straight[m])

        for m in range(micro):
            left(FWD, m, fwd_straight[m])
            left(BWD, m, bwd_straight[m])
            sent(HOME, BWD, m, own_bwd[m])
            sent(AWAY, BWD, m, their_bwd[m])
            if own_fwd[m]:
                relay_sent(FWD, m)
            if own_bwd[m]:
                relay_sent(BWD, m)

    for m in range(micro):
        section_copy(m).wait_send()
    route_copy.wait_send()


def copy_out(out_in, gin_in, gout_in, out_ref, gin_ref, gout_ref, sem):
    pairs = ((gin_in, gin_ref), (gout_in, gout_ref), (out_in, out_ref))
    copies = []
    for i, (a, b) in enumerate(pairs):
        step = a.shape[0] // PARTS[i]
        for j in range(PARTS[i]):
            part = slice(j * step, (j + 1) * step)
            copies.append(pltpu.make_async_copy(a.at[part], b.at[part], sem.at[len(copies)]))
    for copy in copies:
        copy.start()
    for copy in copies:
        copy.wait()


def on_device(boundary, norm_gain, gate_prob, expert_ids, slot_ids, weight_in, weight_out):
    experts = lax.axis_size("expert")
    micro, tok, half = boundary.shape[1:]
    full, hidden_half = weight_in.shape[2:]
    cap = 2 * tok // experts
    pad = -(-cap // 16) * 16
    total = experts * pad
    mid_type = F32 if total <= 512 else BF16
    vmem = pl.BlockSpec(memory_space=pltpu.VMEM)
    anywhere = pl.BlockSpec(memory_space=pl.ANY)
    per_block = pltpu.SemaphoreType.DMA((2, micro, experts))
    per_pair = pltpu.SemaphoreType.DMA((2, micro))
    per_piece = pltpu.SemaphoreType.DMA((2, micro, SPLIT))
    per_micro = pltpu.SemaphoreType.DMA((micro,))
    pieces = pltpu.VMEM((2, micro, total, half), BF16)
    tokens = pltpu.VMEM((micro, tok, half), BF16)
    sums = pltpu.VMEM((micro, max(8, total // tok), tok), F32)
    routes = pltpu.VMEM((8, tok), F32)
    table = pltpu.VMEM((micro, total, tok), BF16)
    out, grad_in, grad_out = pl.pallas_call(
        functools.partial(kernel, experts, cap, pad, RELAYED, DIRECT),
        out_shape=(
            pltpu.VMEM((micro, tok, half), BF16),
            pltpu.VMEM((full, hidden_half), BF16),
            pltpu.VMEM((hidden_half, full), BF16),
        ),
        in_specs=[anywhere] * 7,
        out_specs=(vmem, vmem, vmem),
        scratch_shapes=[
            table,
            table,
            pieces,
            pltpu.VMEM((2, micro * total, full), BF16),
            pltpu.VMEM((micro * total, full), BF16),
            pltpu.VMEM((micro * total, hidden_half), BF16),
            pltpu.VMEM((micro * total, hidden_half), BF16),
            pltpu.VMEM((micro * total, hidden_half), mid_type),
            pltpu.VMEM((micro * total, 1), F32),
            pieces,
            pieces,
            pieces,
            pieces,
            tokens,
            tokens,
            sums,
            sums,
            routes,
            routes,
            pltpu.VMEM((full, hidden_half), BF16),
            pltpu.VMEM((hidden_half, full), BF16),
            tokens,
            pltpu.VMEM((1, full), F32),
            pltpu.VMEM((micro, tok), F32),
            pltpu.VMEM((micro, tok), jnp.int32),
            pltpu.VMEM((micro, tok), jnp.int32),
            pltpu.SemaphoreType.DMA((7,)),
            pltpu.SemaphoreType.REGULAR,
            per_pair, per_block,
            per_pair, per_pair,
            per_piece, per_piece,
            per_pair, per_pair,
            per_micro, per_micro,
            per_micro, per_micro,
            per_pair,
            pltpu.SemaphoreType.DMA,
            pltpu.SemaphoreType.DMA,
        ],
        compiler_params=pltpu.CompilerParams(
            collective_id=0, has_side_effects=True, vmem_limit_bytes=VMEM_LIMIT
        ),
    )(
        boundary[0], norm_gain, gate_prob[0], expert_ids[0], slot_ids[0],
        weight_in[0, 0], weight_out[0, 0],
    )
    results = (out, grad_in, grad_out)
    out, grad_in, grad_out = pl.pallas_call(
        copy_out,
        out_shape=[jax.ShapeDtypeStruct(x.shape, x.dtype) for x in results],
        in_specs=[vmem] * 3,
        out_specs=[anywhere] * 3,
        scratch_shapes=[pltpu.SemaphoreType.DMA((sum(PARTS),))],
        compiler_params=pltpu.CompilerParams(vmem_limit_bytes=COPY_LIMIT),
    )(*results)
    return (out[None], grad_in[None, None], grad_out[None, None])


def solution(mesh):
    placed = (
        P("section", None, "expert", "head"),
        P("section", None),
        P("section", None, "expert"),
        P("section", None, "expert"),
        P("section", None, "expert"),
        P("section", "expert", None, "head"),
        P("section", "expert", "head", None),
    )
    return jax.shard_map(
        on_device,
        mesh=mesh,
        in_specs=placed,
        out_specs=(
            P("section", None, "expert", "head"),
            P("section", "expert", None, "head"),
            P("section", "expert", "head", None),
        ),
        check_vma=False,
    )
```

```python
import functools

import jax
import jax.numpy as jnp
from jax import lax
from jax.experimental import pallas as pl
from jax.experimental.pallas import tpu as pltpu
from jax.sharding import PartitionSpec as P

EPSILON = 1e-06
ROOT_COEF = 0.7978845608
CUBE_COEF = 0.044715
MESH = pl.DeviceIdType.MESH
BF16 = jnp.bfloat16
F32 = jnp.float32
FWD, BWD = 0, 1
COLS = 256
SPLIT = 2
VMEM_LIMIT = 56 * 2**20
COPY_LIMIT = 2**20
RELAYED = {"f0": (True, True), "b1": (True, True), "f1": (True, False), "b0": (True, False)}
DIRECT = {"f0": (True, True), "b1": (True, False), "f1": (False, False), "b0": (False, True)}
RELAY_NEAR = True
TURN_AT = 0
HOLD = 1
TAIL = 7
PARTS = (4, 4, 1)
ORDER = 3
UNROLL = 6
PUMP_AT = 0


def activate(pre_act):
    tangent = jnp.tanh(ROOT_COEF * (pre_act + CUBE_COEF * pre_act * pre_act * pre_act))
    act_value = 0.5 * pre_act * (1.0 + tangent)
    act_slope = 0.5 * (1.0 + tangent) + 0.5 * pre_act * (1.0 - tangent * tangent) * ROOT_COEF * (
        1.0 + 3.0 * CUBE_COEF * pre_act * pre_act
    )
    return (act_value, act_slope)


def dot(left, right, dims=((1,), (0,))):
    return lax.dot_general(left, right, (dims, ((), ())), preferred_element_type=F32)


NT = ((1,), (1,))
TN = ((0,), (0,))


def kernel(
    experts, cap, pad, relayed, direct,
    local_hbm, gain_hbm, prob_hbm, ids_hbm, slots_hbm, win_hbm, wout_hbm,
    out_ref, gin_ref, gout_ref,
    tab, tab2, send, rows, normed, act, gpre, mid, inv_ref, keep, away, recvp, back,
    sec_src, sec_in, xsend, xrecv, route, route_in, win_ref, wout_ref,
    local_ref, gain_ref, prob_ref, ids_ref, slots_ref, load_sem, turn,
    s1, r1, s2, r2, s3, r3, s4, r4, s5, r5, s6, r6, s7, s8, r8,
):
    small = [
        pltpu.make_async_copy(source, target, load_sem.at[2 + i])
        for i, (source, target) in enumerate(
            (
                (local_hbm, local_ref),
                (gain_hbm, gain_ref),
                (prob_hbm, prob_ref),
                (ids_hbm, ids_ref),
                (slots_hbm, slots_ref),
            )
        )
    ]
    win_load = pltpu.make_async_copy(win_hbm, win_ref, load_sem.at[0])
    wout_load = pltpu.make_async_copy(wout_hbm, wout_ref, load_sem.at[1])
    sec, me, head = lax.axis_index("section"), lax.axis_index("expert"), lax.axis_index("head")
    other = 1 - head
    upper = lax.div(2 * me, experts)
    micro, tok, half = local_ref.shape
    full = 2 * half
    total = experts * pad
    groups = total // tok
    piece_rows = total // SPLIT
    hidden_half = win_ref.shape[1]
    chunks = hidden_half // COLS
    own_cols = pl.ds(pl.multiple_of(head * half, 128), half)
    other_cols = pl.ds(pl.multiple_of(other * half, 128), half)

    barrier = pltpu.get_barrier_semaphore()

    def greet(k, carry):
        d = lax.rem(me + k, experts)
        for h in range(2):
            pl.semaphore_signal(
                barrier, inc=1, device_id={"expert": d, "head": h}, device_id_type=MESH
            )
        return carry

    lax.fori_loop(1, experts, greet, 0)
    pl.semaphore_signal(barrier, inc=1, device_id={"head": other}, device_id_type=MESH)
    pl.semaphore_signal(barrier, inc=1, device_id={"section": 1 - sec}, device_id_type=MESH)
    for load in small:
        load.start()
    win_load.start()
    wout_load.start()
    for load in small:
        load.wait()

    def far_first(k):
        return k * upper + (experts - 1 - k) * (1 - upper)

    def near_first(k):
        return far_first(experts - 1 - k)

    def each(order, action, with_me, lo=0, hi=experts):
        def step(k, carry):
            d = order(k)
            if with_me:
                action(d)
            else:
                pl.when(d != me)(lambda: action(d))
            return carry

        lax.fori_loop(lo, hi, step, 0)

    def slot_rows(index):
        return pl.ds(pl.multiple_of(index * pad, pad), pad)

    def micro_rows(m, index):
        return pl.ds(pl.multiple_of(m * total + index * pad, pad), pad)

    def span(m):
        return slice(m * total, (m + 1) * total)

    eye = lax.broadcasted_iota(jnp.int32, (tok, tok), 0) == lax.broadcasted_iota(
        jnp.int32, (tok, tok), 1
    )

    def to_col(row):
        return jnp.sum(jnp.where(eye, row, 0.0), axis=1, keepdims=True)

    def to_row(col):
        return jnp.sum(jnp.where(eye, col, 0.0), axis=0, keepdims=True)

    def fill_tab(ref, m, target):
        place_of = lax.broadcasted_iota(jnp.int32, (total, tok), 0).astype(F32)
        ref[m] = jnp.where(target == place_of, 1.0, 0.0).astype(BF16)

    for m in range(micro):
        ids, slots = ids_ref[m : m + 1, :], slots_ref[m : m + 1, :]
        target = jnp.where(slots < cap, ids * pad + slots, -1).astype(F32)
        fill_tab(tab, m, target)
        route[m : m + 1, :] = target
        route[micro + m : micro + m + 1, :] = prob_ref[m : m + 1, :]
    prob = [to_col(prob_ref[m : m + 1, :]) for m in range(micro)]
    gain = gain_ref[...]

    route_copy = pltpu.make_async_remote_copy(
        src_ref=route,
        dst_ref=route_in,
        send_sem=s8,
        recv_sem=r8,
        device_id={"section": 1 - sec},
        device_id_type=MESH,
    )

    def route_done():
        route_copy.wait_recv()
        for m in range(micro):
            fill_tab(tab2, m, route_in[m : m + 1, :])

    HOME, AWAY = 0, 1

    def target_section(slot):
        return sec if slot == HOME else 1 - sec

    def chunk_copy(slot, kind, m, dst, came_from):
        return pltpu.make_async_remote_copy(
            src_ref=send.at[slot, m, slot_rows(dst), :],
            dst_ref=rows.at[kind, micro_rows(m, came_from), own_cols],
            send_sem=s1.at[slot, m],
            recv_sem=r1.at[kind, m, came_from],
            device_id={"section": target_section(slot), "expert": dst},
            device_id_type=MESH,
        )

    def cross_copy(slot, kind, m, dst, came_from, cols):
        return pltpu.make_async_remote_copy(
            src_ref=send.at[slot, m, slot_rows(dst), :],
            dst_ref=rows.at[kind, micro_rows(m, came_from), cols],
            send_sem=s2.at[slot, m],
            recv_sem=r2.at[kind, m],
            device_id={"section": target_section(slot), "expert": dst, "head": other},
            device_id_type=MESH,
        )

    def relay_copy(kind, m, block, cols):
        return pltpu.make_async_remote_copy(
            src_ref=rows.at[kind, micro_rows(m, block), cols],
            dst_ref=rows.at[kind, micro_rows(m, block), cols],
            send_sem=s7.at[kind, m],
            recv_sem=r2.at[kind, m],
            device_id={"head": other},
            device_id_type=MESH,
        )

    def place(slot, m, tokens):
        table = tab if slot == HOME else tab2
        send[slot, m] = dot(table[m], tokens).astype(BF16)

    def dispatch(slot, kind, m, relay):
        def both_heads(d):
            chunk_copy(slot, kind, m, d, me).start()
            if not relay:
                cross_copy(slot, kind, m, d, me, own_cols).start()

        each(near_first if relay and RELAY_NEAR else far_first, both_heads, slot == AWAY)
        if slot == HOME:
            rows[kind, micro_rows(m, me), own_cols] = send[slot, m, slot_rows(me), :]
            if not relay:
                cross_copy(slot, kind, m, me, me, own_cols).start()

    def pump(slot, kind, m, relay):
        def one(block):
            chunk_copy(slot, kind, m, block, block).wait_recv()
            if relay:
                relay_copy(kind, m, block, own_cols).start()

        if slot == HOME and relay:
            relay_copy(kind, m, me, own_cols).start()
        each(near_first, one, slot == AWAY)

    def arrived(kind, m):
        relayed_blocks(kind, m, other_cols).wait_recv()

    def sent(slot, kind, m, relay):
        blocks = experts if slot == AWAY else experts - 1
        pltpu.make_async_remote_copy(
            src_ref=send.at[slot, m, 0 : blocks * pad, :],
            dst_ref=rows.at[kind, 0 : blocks * pad, own_cols],
            send_sem=s1.at[slot, m],
            recv_sem=r1.at[kind, m, 0],
            device_id={"head": other},
            device_id_type=MESH,
        ).wait_send()
        if not relay:
            pltpu.make_async_remote_copy(
                src_ref=send.at[slot, m],
                dst_ref=rows.at[kind, 0:total, own_cols],
                send_sem=s2.at[slot, m],
                recv_sem=r2.at[kind, m],
                device_id={"head": other},
                device_id_type=MESH,
            ).wait_send()

    def relayed_blocks(kind, m, cols):
        return pltpu.make_async_remote_copy(
            src_ref=rows.at[kind, span(m), cols],
            dst_ref=rows.at[kind, span(m), cols],
            send_sem=s7.at[kind, m],
            recv_sem=r2.at[kind, m],
            device_id={"head": other},
            device_id_type=MESH,
        )

    def relay_sent(kind, m):
        relayed_blocks(kind, m, own_cols).wait_send()

    def piece_at(c):
        p = c * upper + (SPLIT - 1 - c) * (1 - upper)
        return p, pl.ds(pl.multiple_of(p * piece_rows, piece_rows), piece_rows)

    def away_copy(kind, m, c):
        _, part = piece_at(c)
        return pltpu.make_async_remote_copy(
            src_ref=away.at[kind, m, part, :],
            dst_ref=recvp.at[kind, m, part, :],
            send_sem=s3.at[kind, m, c],
            recv_sem=r3.at[kind, m, c],
            device_id={"head": other},
            device_id_type=MESH,
        )

    def back_copy(kind, m, dst, came_from):
        return pltpu.make_async_remote_copy(
            src_ref=keep.at[kind, m, slot_rows(dst), :],
            dst_ref=back.at[kind, m, slot_rows(came_from), :],
            send_sem=s4.at[kind, m],
            recv_sem=r4.at[kind, m],
            device_id={"expert": dst},
            device_id_type=MESH,
        )

    def straight_copy(kind, m, dst, came_from):
        return pltpu.make_async_remote_copy(
            src_ref=away.at[kind, m, slot_rows(dst), :],
            dst_ref=recvp.at[kind, m, slot_rows(came_from), :],
            send_sem=s3.at[kind, m, 0],
            recv_sem=r3.at[kind, m, 0],
            device_id={"expert": dst, "head": other},
            device_id_type=MESH,
        )

    def straight_blocks(kind, m):
        return pltpu.make_async_remote_copy(
            src_ref=away.at[kind, m],
            dst_ref=recvp.at[kind, m],
            send_sem=s3.at[kind, m, 0],
            recv_sem=r3.at[kind, m, 0],
            device_id={"head": other},
            device_id_type=MESH,
        )

    def piece_blocks(c):
        return c * experts // SPLIT, (c + 1) * experts // SPLIT

    def send_straight(kind, m, lo, hi):
        each(far_first, lambda dst: straight_copy(kind, m, dst, me).start(), True, lo, hi)

    def send_same(kind, m, lo, hi):
        each(far_first, lambda dst: back_copy(kind, m, dst, me).start(), False, lo, hi)

    def keep_own(kind, m):
        back[kind, m, slot_rows(me), :] = keep[kind, m, slot_rows(me), :]

    def back_blocks(kind, m):
        return pltpu.make_async_remote_copy(
            src_ref=keep.at[kind, m, 0 : (experts - 1) * pad, :],
            dst_ref=back.at[kind, m, 0 : (experts - 1) * pad, :],
            send_sem=s4.at[kind, m],
            recv_sem=r4.at[kind, m],
            device_id={"head": other},
            device_id_type=MESH,
        )

    def send_back(kind, m):
        if kind == BWD:
            sum_copy(m).wait_recv()
        for c in range(SPLIT):
            p, part = piece_at(c)
            away_copy(kind, m, c).wait_recv()
            if kind == FWD:
                summed = keep[kind, m, part, :].astype(F32) + recvp[kind, m, part, :].astype(F32)
                keep[kind, m, part, :] = summed.astype(BF16)
            else:
                for i in range(groups // SPLIT):
                    g = p * (groups // SPLIT) + i
                    here = pl.ds(pl.multiple_of(g * tok, tok), tok)
                    there = pl.ds(pl.multiple_of(m * total + g * tok, tok), tok)
                    cross = to_col(xsend[m, pl.ds(g, 1), :] + xrecv[m, pl.ds(g, 1), :])
                    inv = inv_ref[there, :]
                    grad = keep[kind, m, here, :].astype(F32) + recvp[kind, m, here, :].astype(F32)
                    values = rows[FWD, there, own_cols].astype(F32)
                    delta = inv * (gain_ref[:, own_cols] * grad) - values * (
                        inv * inv * inv * cross / full
                    )
                    keep[kind, m, here, :] = delta.astype(BF16)
            send_same(kind, m, *piece_blocks(c))
        keep_own(kind, m)

    def collect(kind, m, straight):
        back_blocks(kind, m).wait_recv()
        found = dot(tab[m], back[kind, m], TN)
        if straight:
            straight_blocks(kind, m).wait_recv()
            found = found + dot(tab[m], recvp[kind, m], TN)
        return found

    def section_copy(m):
        return pltpu.make_async_remote_copy(
            src_ref=sec_src.at[m],
            dst_ref=sec_in.at[m],
            send_sem=s5.at[m],
            recv_sem=r5.at[m],
            device_id={"section": 1 - sec},
            device_id_type=MESH,
        )

    def sum_copy(m):
        return pltpu.make_async_remote_copy(
            src_ref=xsend.at[m],
            dst_ref=xrecv.at[m],
            send_sem=s6.at[m],
            recv_sem=r6.at[m],
            device_id={"head": other},
            device_id_type=MESH,
        )

    def normalize(m):
        values = rows[FWD, span(m), :].astype(F32)
        inv_scale = lax.rsqrt(jnp.mean(values * values, axis=-1, keepdims=True) + EPSILON)
        inv_ref[span(m), :] = inv_scale
        normed[span(m), :] = (values * inv_scale * gain).astype(BF16)

    def each_chunk(action):
        def step(c, carry):
            action(pl.ds(pl.multiple_of(c * COLS, COLS), COLS))
            return carry

        lax.fori_loop(0, chunks, step, 0, unroll=UNROLL if total <= 512 else 1)

    def out_partial(m, straight):
        away[FWD, m] = dot(act[span(m), :], wout_ref[:, other_cols]).astype(BF16)
        if straight:
            send_straight(FWD, m, 0, experts)
        else:
            for c in range(SPLIT):
                away_copy(FWD, m, c).start()
        keep[FWD, m] = dot(act[span(m), :], wout_ref[:, own_cols]).astype(BF16)
        if straight:
            send_same(FWD, m, 0, experts)
            keep_own(FWD, m)

    def grad_straight(m):
        away[BWD, m] = dot(gpre[span(m), :], win_ref[other_cols, :], NT).astype(BF16)
        keep[BWD, m] = dot(gpre[span(m), :], win_ref[own_cols, :], NT).astype(BF16)
        sides = ((away, other_cols), (keep, own_cols))
        for c in range(SPLIT):
            p, _ = piece_at(c)
            for i in range(groups // SPLIT):
                g = p * (groups // SPLIT) + i
                here = pl.ds(pl.multiple_of(g * tok, tok), tok)
                there = pl.ds(pl.multiple_of(m * total + g * tok, tok), tok)
                scaled = [ref[BWD, m, here, :].astype(F32) * gain_ref[:, cols] for ref, cols in sides]
                values = [rows[FWD, there, cols].astype(F32) for _, cols in sides]
                cross = jnp.sum(
                    scaled[0] * values[0] + scaled[1] * values[1], axis=1, keepdims=True
                )
                inv = inv_ref[there, :]
                cubed = inv * inv * inv * cross / full
                for (ref, _), part, value in zip(sides, scaled, values):
                    ref[BWD, m, here, :] = (inv * part - value * cubed).astype(BF16)
            send_straight(BWD, m, *piece_blocks(c))
            send_same(BWD, m, *piece_blocks(c))
        keep_own(BWD, m)

    def grad_partial(m, straight):
        if straight:
            grad_straight(m)
            return
        away[BWD, m] = dot(gpre[span(m), :], win_ref[other_cols, :], NT).astype(BF16)
        for c in range(SPLIT):
            away_copy(BWD, m, c).start()
        keep[BWD, m] = dot(gpre[span(m), :], win_ref[own_cols, :], NT).astype(BF16)
        for g in range(groups):
            here = slice(g * tok, (g + 1) * tok)
            there = slice(m * total + g * tok, m * total + (g + 1) * tok)
            cross = jnp.zeros((tok, 1), F32)
            for ref, cols in ((away, other_cols), (keep, own_cols)):
                scaled = ref[BWD, m, here, :].astype(F32) * gain_ref[:, cols]
                cross = cross + jnp.sum(
                    scaled * rows[FWD, there, cols].astype(F32), axis=1, keepdims=True
                )
            xsend[m, g : g + 1, :] = to_row(cross)
        sum_copy(m).start()

    def layer_out(m, tokens, straight):
        return (tokens.astype(F32) + prob[m] * collect(FWD, m, straight)).astype(BF16)

    def sent_grad(weight, cot):
        return (weight * cot.astype(F32)).astype(BF16)

    def layer_grad(m, cot, straight):
        return (cot.astype(F32) + collect(BWD, m, straight)).astype(BF16)

    def left(kind, m, straight):
        back_blocks(kind, m).wait_send()
        if straight:
            straight_blocks(kind, m).wait_send()
            return
        for c in range(SPLIT):
            away_copy(kind, m, c).wait_send()
        if kind == BWD:
            sum_copy(m).wait_send()

    def in_grads():
        def first(c, carry):
            part = pl.ds(pl.multiple_of(c * COLS, COLS), COLS)
            gin_ref[part, :] = dot(normed[:, part], gpre[...], TN).astype(BF16)
            return carry

        lax.fori_loop(0, full // COLS, first, 0, unroll=3 if total <= 512 else 1)

    def out_grads():
        def second(part):
            gout_ref[part, :] = dot(act[:, part], rows[BWD], TN).astype(BF16)

        each_chunk(second)

    @pl.when(sec == 0)
    def _():
        own_fwd, own_bwd, their_fwd = relayed["f0"], relayed["b0"], relayed["f1"]
        fwd_straight, bwd_straight = direct["f0"], direct["b0"]
        for m in range(micro):
            place(HOME, m, local_ref[m])
        pl.semaphore_wait(barrier, 2 * experts)
        dispatch(HOME, FWD, 0, own_fwd[0])
        if own_fwd[1]:
            dispatch(HOME, FWD, 1, own_fwd[1])
        route_copy.start()
        win_load.wait()
        wout_load.wait()
        pump(HOME, FWD, 0, own_fwd[0])

        def signal_turn():
            pl.semaphore_signal(turn, inc=1, device_id={"section": 1 - sec}, device_id_type=MESH)

        if TURN_AT == 0:
            signal_turn()
        if PUMP_AT == 0 and own_fwd[1]:
            pump(HOME, FWD, 1, own_fwd[1])

        def forward(m):
            arrived(FWD, m)
            if m == 0 and TURN_AT == 1:
                signal_turn()
            if m == 0 and not own_fwd[1]:
                dispatch(HOME, FWD, 1, own_fwd[1])
            normalize(m)

            def chunk(part):
                pre = dot(normed[span(m), :], win_ref[:, part])
                value, slope = activate(pre)
                act[span(m), part] = value.astype(BF16)
                mid[span(m), part] = slope.astype(mid.dtype)

            each_chunk(chunk)

        def hidden(m):
            sec_src[m] = layer_out(m, local_ref[m], fwd_straight[m])
            place(AWAY, m, sec_src[m])
            dispatch(AWAY, FWD, m, their_fwd[m])
            section_copy(m).start()

        forward(0)
        if PUMP_AT == 1 and own_fwd[1]:
            pump(HOME, FWD, 1, own_fwd[1])
        out_partial(0, fwd_straight[0])
        route_done()
        if not own_fwd[1]:
            pump(HOME, FWD, 1, own_fwd[1])
        forward(1)
        if not fwd_straight[0]:
            send_back(FWD, 0)
        if HOLD == 1:
            signal_turn()
        out_partial(1, fwd_straight[1])
        hidden(0)
        if HOLD == 2:
            signal_turn()
        if not fwd_straight[1]:
            send_back(FWD, 1)
        hidden(1)

        def backward(m):
            pump(AWAY, BWD, m, own_bwd[m])
            arrived(BWD, m)

            def chunk(part):
                grad_act = dot(rows[BWD, span(m), :], wout_ref[part, :], NT)
                gpre[span(m), part] = (grad_act * mid[span(m), part].astype(F32)).astype(BF16)

            each_chunk(chunk)

        backward(0)
        grad_partial(0, bwd_straight[0])
        backward(1)
        if not bwd_straight[0]:
            send_back(BWD, 0)
        grad_partial(1, bwd_straight[1])
        out_grads()
        if not bwd_straight[1]:
            send_back(BWD, 1)
        in_grads()
        section_copy(0).wait_recv()
        out_ref[0] = layer_grad(0, sec_in[0], bwd_straight[0])
        section_copy(1).wait_recv()
        out_ref[1] = layer_grad(1, sec_in[1], bwd_straight[1])

        for m in range(micro):
            left(FWD, m, fwd_straight[m])
            left(BWD, m, bwd_straight[m])
            sent(HOME, FWD, m, own_fwd[m])
            sent(AWAY, FWD, m, their_fwd[m])
            if own_fwd[m]:
                relay_sent(FWD, m)
            if own_bwd[m]:
                relay_sent(BWD, m)

    @pl.when(sec != 0)
    def _():
        own_bwd, own_fwd, their_bwd = relayed["b1"], relayed["f1"], relayed["b0"]
        fwd_straight, bwd_straight = direct["f1"], direct["b1"]
        for m in range(micro):
            place(HOME, m, sent_grad(prob[m], local_ref[m]))
        pl.semaphore_wait(barrier, 2 * experts)
        route_copy.start()
        win_load.wait()
        wout_load.wait()

        pl.semaphore_wait(turn, 1)
        for m in range(micro):
            dispatch(HOME, BWD, m, own_bwd[m])
        if HOLD:
            pl.semaphore_wait(turn, 1)
        for m in range(micro):
            pump(HOME, BWD, m, own_bwd[m])

        def early_grad(m):
            arrived(BWD, m)

            def early(part):
                grad_act = dot(rows[BWD, span(m), :], wout_ref[part, :], NT)
                mid[span(m), part] = grad_act.astype(mid.dtype)

            each_chunk(early)

        early_grad(0)
        route_done()
        prob_in = [to_col(route_in[micro + m : micro + m + 1, :]) for m in range(micro)]
        early_grad(1)

        def both(m):
            arrived(FWD, m)
            normalize(m)

            def chunk(part):
                pre = dot(normed[span(m), :], win_ref[:, part])
                value, slope = activate(pre)
                act[span(m), part] = value.astype(BF16)
                gpre[span(m), part] = (mid[span(m), part].astype(F32) * slope).astype(BF16)

            each_chunk(chunk)

        def finish(m):
            sec_src[m] = layer_grad(m, local_ref[m], bwd_straight[m])
            place(AWAY, m, sent_grad(prob_in[m], sec_src[m]))
            dispatch(AWAY, BWD, m, their_bwd[m])
            section_copy(m).start()

        pump(AWAY, FWD, 0, own_fwd[0])
        both(0)
        grad_partial(0, bwd_straight[0])
        if not bwd_straight[0]:
            send_back(BWD, 0)
        if ORDER == 1:
            finish(0)
        pump(AWAY, FWD, 1, own_fwd[1])
        both(1)
        if ORDER == 2:
            finish(0)
        grad_partial(1, bwd_straight[1])
        if TAIL == 5 or TAIL == 6:
            out_partial(0, fwd_straight[0])
            out_partial(1, fwd_straight[1])
        if TAIL == 7:
            out_partial(0, fwd_straight[0])
        if ORDER == 3:
            finish(0)
        if not bwd_straight[1]:
            send_back(BWD, 1)
        if TAIL == 7:
            out_partial(1, fwd_straight[1])
        if TAIL == 6:
            in_grads()
        if TAIL == 0:
            out_partial(0, fwd_straight[0])
            out_partial(1, fwd_straight[1])
        if TAIL == 8:
            out_partial(0, fwd_straight[0])
        finish(1)
        if TAIL == 8:
            in_grads()
            out_grads()
            out_partial(1, fwd_straight[1])
        if TAIL == 1:
            out_partial(0, fwd_straight[0])
            out_partial(1, fwd_straight[1])
        if TAIL != 6 and TAIL != 8:
            in_grads()
        if TAIL == 2:
            out_partial(0, fwd_straight[0])
            out_partial(1, fwd_straight[1])
        if TAIL != 8:
            out_grads()
        if TAIL == 3:
            out_partial(0, fwd_straight[0])
            out_partial(1, fwd_straight[1])
        if not fwd_straight[0]:
            send_back(FWD, 0)
        if not fwd_straight[1]:
            send_back(FWD, 1)
        for m in range(micro):
            section_copy(m).wait_recv()
            out_ref[m] = layer_out(m, sec_in[m], fwd_straight[m])

        for m in range(micro):
            left(FWD, m, fwd_straight[m])
            left(BWD, m, bwd_straight[m])
            sent(HOME, BWD, m, own_bwd[m])
            sent(AWAY, BWD, m, their_bwd[m])
            if own_fwd[m]:
                relay_sent(FWD, m)
            if own_bwd[m]:
                relay_sent(BWD, m)

    for m in range(micro):
        section_copy(m).wait_send()
    route_copy.wait_send()


def copy_out(out_in, gin_in, gout_in, out_ref, gin_ref, gout_ref, sem):
    pairs = ((gin_in, gin_ref), (gout_in, gout_ref), (out_in, out_ref))
    copies = []
    for i, (a, b) in enumerate(pairs):
        step = a.shape[0] // PARTS[i]
        for j in range(PARTS[i]):
            part = slice(j * step, (j + 1) * step)
            copies.append(pltpu.make_async_copy(a.at[part], b.at[part], sem.at[len(copies)]))
    for copy in copies:
        copy.start()
    for copy in copies:
        copy.wait()


def on_device(boundary, norm_gain, gate_prob, expert_ids, slot_ids, weight_in, weight_out):
    experts = lax.axis_size("expert")
    micro, tok, half = boundary.shape[1:]
    full, hidden_half = weight_in.shape[2:]
    cap = 2 * tok // experts
    pad = -(-cap // 16) * 16
    total = experts * pad
    mid_type = F32 if total <= 512 else BF16
    vmem = pl.BlockSpec(memory_space=pltpu.VMEM)
    anywhere = pl.BlockSpec(memory_space=pl.ANY)
    per_block = pltpu.SemaphoreType.DMA((2, micro, experts))
    per_pair = pltpu.SemaphoreType.DMA((2, micro))
    per_piece = pltpu.SemaphoreType.DMA((2, micro, SPLIT))
    per_micro = pltpu.SemaphoreType.DMA((micro,))
    pieces = pltpu.VMEM((2, micro, total, half), BF16)
    tokens = pltpu.VMEM((micro, tok, half), BF16)
    sums = pltpu.VMEM((micro, max(8, total // tok), tok), F32)
    routes = pltpu.VMEM((8, tok), F32)
    table = pltpu.VMEM((micro, total, tok), BF16)
    out, grad_in, grad_out = pl.pallas_call(
        functools.partial(kernel, experts, cap, pad, RELAYED, DIRECT),
        out_shape=(
            pltpu.VMEM((micro, tok, half), BF16),
            pltpu.VMEM((full, hidden_half), BF16),
            pltpu.VMEM((hidden_half, full), BF16),
        ),
        in_specs=[anywhere] * 7,
        out_specs=(vmem, vmem, vmem),
        scratch_shapes=[
            table,
            table,
            pieces,
            pltpu.VMEM((2, micro * total, full), BF16),
            pltpu.VMEM((micro * total, full), BF16),
            pltpu.VMEM((micro * total, hidden_half), BF16),
            pltpu.VMEM((micro * total, hidden_half), BF16),
            pltpu.VMEM((micro * total, hidden_half), mid_type),
            pltpu.VMEM((micro * total, 1), F32),
            pieces,
            pieces,
            pieces,
            pieces,
            tokens,
            tokens,
            sums,
            sums,
            routes,
            routes,
            pltpu.VMEM((full, hidden_half), BF16),
            pltpu.VMEM((hidden_half, full), BF16),
            tokens,
            pltpu.VMEM((1, full), F32),
            pltpu.VMEM((micro, tok), F32),
            pltpu.VMEM((micro, tok), jnp.int32),
            pltpu.VMEM((micro, tok), jnp.int32),
            pltpu.SemaphoreType.DMA((7,)),
            pltpu.SemaphoreType.REGULAR,
            per_pair, per_block,
            per_pair, per_pair,
            per_piece, per_piece,
            per_pair, per_pair,
            per_micro, per_micro,
            per_micro, per_micro,
            per_pair,
            pltpu.SemaphoreType.DMA,
            pltpu.SemaphoreType.DMA,
        ],
        compiler_params=pltpu.CompilerParams(
            collective_id=0, has_side_effects=True, vmem_limit_bytes=VMEM_LIMIT
        ),
    )(
        boundary[0], norm_gain, gate_prob[0], expert_ids[0], slot_ids[0],
        weight_in[0, 0], weight_out[0, 0],
    )
    results = (out, grad_in, grad_out)
    out, grad_in, grad_out = pl.pallas_call(
        copy_out,
        out_shape=[jax.ShapeDtypeStruct(x.shape, x.dtype) for x in results],
        in_specs=[vmem] * 3,
        out_specs=[anywhere] * 3,
        scratch_shapes=[pltpu.SemaphoreType.DMA((sum(PARTS),))],
        compiler_params=pltpu.CompilerParams(vmem_limit_bytes=COPY_LIMIT),
    )(*results)
    return (out[None], grad_in[None, None], grad_out[None, None])


def solution(mesh):
    placed = (
        P("section", None, "expert", "head"),
        P("section", None),
        P("section", None, "expert"),
        P("section", None, "expert"),
        P("section", None, "expert"),
        P("section", "expert", None, "head"),
        P("section", "expert", "head", None),
    )
    return jax.shard_map(
        on_device,
        mesh=mesh,
        in_specs=placed,
        out_specs=(
            P("section", None, "expert", "head"),
            P("section", "expert", None, "head"),
            P("section", "expert", "head", None),
        ),
        check_vma=False,
    )
```
